256 devices in a mesh: frame: 32 (over z, x), row: 8 (over y, core).
Axes of the slice: x: 4, y: 4, z: 8, core: 2. Of those that a mesh axis runs over, the one named last changes fastest.
Arguments:
- query_tokens: bfloat16 [64, 24, 40, 2240], P('frame', 'row'), may hold values from -6 to 6
- key_tokens: bfloat16 [64, 24, 40, 2240], P('frame', 'row'), may hold values from -6 to 6
- value_tokens: bfloat16 [64, 24, 40, 2240], P('frame', 'row'), may hold values from -6 to 6
- norm_gain: float32 [2240], replicated, may hold values from 0.1 to 1.9
- hidden: bfloat16 [64, 24, 40, 11200], P('frame', 'row'), may hold values from -6 to 6
- time_weight: float32 [2, 11200], replicated, may hold values from -4 to 4
- space_weight: float32 [3, 3, 11200], replicated, may hold values from -2 to 2
- conv_bias: float32 [11200], replicated, may hold values from -3 to 3
Outputs:
- attention: bfloat16 [64, 24, 40, 2240], P('frame', 'row')
- ffn_out: bfloat16 [64, 24, 40, 5600], P('frame', 'row')
The draws below stay inside these ranges and needn't reach their ends.
All inputs are finite; a program needn't handle non-finite values.
Results may differ from the reference program's by a relative error of at most 0.0056.
Values may be sent and summed in bfloat16 or wider, within the bound.
No kernel may reach another device: no remote copies, remote signals or barrier semaphores. Data moves between devices by JAX's collectives and lax.ppermute only.
A program may use at most 128 MiB of HBM per device.

```python
import jax
import jax.numpy as jnp
from jax import lax

D = 2240
HD = 112
FF = 5600
COLS = 40
GROUP = 2
FRAMES = 64
ROWS = 24


def block_levels(key, shape, pieces, least, top_value):
    def one(axis_at, shards_of):
        draws = jax.random.uniform(jax.random.fold_in(jax.random.fold_in(key, 6), axis_at), (shards_of,), jnp.float32, least / len(pieces), top_value / len(pieces))
        return jnp.repeat(jnp.exp(draws), shape[axis_at] // shards_of).reshape((-1,) + (1,) * (len(shape) - axis_at - 1))

    factor_of = one(*pieces[0])
    for cut in pieces[1:]:
        factor_of = factor_of * one(*cut)
    return factor_of


def centred(rng, extent, scale, limit, cuts=(), held_as=jnp.bfloat16):
    entries = jax.random.normal(rng, extent, jnp.float32) * scale
    if len(cuts) > 0:
        entries = block_levels(rng, extent, cuts, -0.22, 0.18) * entries
    return jnp.clip(entries, min=-limit, max=limit).astype(held_as)


def setup_inputs(seed: int = 0) -> dict:
    key_of = jax.random.split(jax.random.key(seed), 9)
    query_tokens = centred(key_of[0], (FRAMES, ROWS, COLS, D), 1.0, 6.0, ((0, 32), (1, 8)))
    key_tokens = centred(key_of[1], (FRAMES, ROWS, COLS, D), 1.0, 6.0, ((0, 32), (1, 8)))
    value_tokens = centred(key_of[2], (FRAMES, ROWS, COLS, D), 1.0, 6.0, ((0, 32), (1, 8)))
    norm_gain = jnp.clip(1.0 + 0.18 * jax.random.normal(key_of[3], (D,), jnp.float32), 0.1, 1.9)
    hidden = centred(key_of[4], (FRAMES, ROWS, COLS, 2 * FF), 1.0, 6.0, ((0, 32), (1, 8)))
    time_weight = centred(key_of[5], (2, 2 * FF), 2 ** -0.5, 4.0, (), jnp.float32)
    space_weight = centred(key_of[6], (3, 3, 2 * FF), 9 ** -0.5, 2.0, (), jnp.float32)
    conv_bias = centred(key_of[7], (2 * FF,), 0.5, 3.0, (), jnp.float32)
    return {"query_tokens": query_tokens, "key_tokens": key_tokens, "value_tokens": value_tokens, "norm_gain": norm_gain, "hidden": hidden, "time_weight": time_weight, "space_weight": space_weight, "conv_bias": conv_bias}


epsilon = 1e-06

def reference(query_tokens, key_tokens, value_tokens, norm_gain, hidden, time_weight, space_weight, conv_bias):
    frame_total, row_total, columns, model_width = query_tokens.shape
    head_count = model_width // HD
    block_count = frame_total // GROUP
    tok_count = GROUP * row_total * columns
    query_blocks = query_tokens.reshape(block_count, tok_count, head_count, HD)
    key_blocks = key_tokens.reshape(block_count, tok_count, head_count, HD)
    value_blocks = value_tokens.reshape(block_count, tok_count, head_count, HD)
    gain_heads = norm_gain.reshape(head_count, HD)

    def advance(kv_carry, slices_in):
        query_part, key_part, value_part = slices_in
        key_feat = jnp.maximum(key_part.astype(jnp.float32), 0.0)
        kv_carry = kv_carry + jnp.einsum('thd,the->hde', key_feat, value_part.astype(jnp.float32))
        rounded = lax.optimization_barrier(kv_carry.astype(jnp.bfloat16)).astype(jnp.float32)
        query_feat = jnp.maximum(query_part.astype(jnp.float32), 0.0)
        mixed = jnp.einsum('thd,hde->the', query_feat, rounded)
        mean_square = lax.optimization_barrier(jnp.mean(mixed * mixed, axis=-1, keepdims=True))
        normed = mixed * lax.rsqrt(mean_square + epsilon) * gain_heads
        return (kv_carry, normed.astype(jnp.bfloat16))
    start_state = jnp.zeros((head_count, HD, HD), jnp.float32)
    _, result_blocks = lax.scan(advance, start_state, (query_blocks, key_blocks, value_blocks))
    attention = result_blocks.reshape(frame_total, row_total, columns, model_width)

    def one_frame(frame_index):
        current = lax.dynamic_index_in_dim(hidden, frame_index, 0, keepdims=False).astype(jnp.float32)
        earlier = lax.dynamic_index_in_dim(hidden, jnp.maximum(frame_index - 1, 0).astype(jnp.int32), 0, keepdims=False).astype(jnp.float32)
        earlier = jnp.where(frame_index > 0, earlier, 0.0)
        blended = time_weight[0] * current + time_weight[1] * earlier
        blended = lax.optimization_barrier(blended.astype(jnp.bfloat16)).astype(jnp.float32)
        padded = jnp.pad(blended, ((1, 1), (1, 1), (0, 0)))
        summed = conv_bias + jnp.zeros(blended.shape, jnp.float32)
        for row_off in range(3):
            for col_off in range(3):
                summed = summed + space_weight[row_off, col_off] * padded[row_off:row_off + row_total, col_off:col_off + columns]
        return (summed[..., :FF] * jax.nn.silu(summed[..., FF:])).astype(jnp.bfloat16)
    ffn_out = lax.map(one_frame, jnp.arange(frame_total, dtype=jnp.int32))
    return (attention, ffn_out)
```

```python
import functools

import jax
import jax.numpy as jnp
from jax import lax
from jax.experimental import pallas as pl
from jax.experimental.pallas import tpu as pltpu
from jax.sharding import Mesh, PartitionSpec as P

HD = 112
FF = 5600
LANES = 128
UNIT = 16
SHARES = 8
SHARE_ROWS = 256
INNER = 4
BLOCK = 11 * LANES
epsilon = 1e-06


def windows(width):
    out = []
    for head in range(width // HD):
        tile, offset = divmod(head * HD, LANES)
        span = LANES if offset + HD <= LANES else 2 * LANES
        out.append((tile, offset, min(span, width - tile * LANES)))
    return out


def unit_row(unit, row):
    share, inside = divmod(unit, UNIT)
    return pl.multiple_of((share ^ row) * SHARE_ROWS + inside * UNIT, UNIT)


def partial_kernel(row_ref, key_ref, value_ref, out_ref):
    row = row_ref[0]
    width = key_ref.shape[1]
    pending = {}

    def flush(tile):
        rounded = pending.pop(tile).astype(jnp.bfloat16)
        for piece in range(HD // UNIT):
            out_ref[pl.ds(unit_row(tile * (HD // UNIT) + piece, row), UNIT), :] = rounded[
                piece * UNIT : (piece + 1) * UNIT
            ]

    for tile, offset, span in windows(width):
        lanes = slice(tile * LANES, tile * LANES + span)
        keys = jnp.maximum(key_ref[:, lanes], 0)
        product = lax.dot_general(
            keys, value_ref[:, lanes], (((0,), (0,)), ((), ())), preferred_element_type=jnp.float32
        )
        block = product[offset : offset + HD]
        lane = lax.broadcasted_iota(jnp.int32, block.shape, 1)
        block = jnp.where((lane >= offset) & (lane < offset + HD), block, 0.0)
        for old in [done for done in pending if done < tile]:
            flush(old)
        for step in range(pl.cdiv(span, LANES)):
            part = block[:, step * LANES : min(span, (step + 1) * LANES)]
            if part.shape[1] < LANES:
                part = jnp.concatenate(
                    [part, jnp.zeros((HD, LANES - part.shape[1]), jnp.float32)], axis=1
                )
            at = tile + step
            pending[at] = pending[at] + part if at in pending else part
    tiles = max(pending) + 1
    for old in sorted(pending):
        flush(old)
    for unit in range(tiles * (HD // UNIT), SHARES * UNIT):
        out_ref[pl.ds(unit_row(unit, row), UNIT), :] = jnp.zeros((UNIT, LANES), jnp.bfloat16)


def mixed_kernel(row_ref, query_ref, state_ref, gain_ref, out_ref):
    row = row_ref[0]
    tokens, width = query_ref.shape
    pending = {}

    def state_tile(tile):
        return jnp.concatenate(
            [
                state_ref[pl.ds(unit_row(tile * (HD // UNIT) + piece, row), UNIT), :]
                for piece in range(HD // UNIT)
            ],
            axis=0,
        )

    def flush(tile):
        lanes = slice(tile * LANES, min(width, (tile + 1) * LANES))
        count = lanes.stop - lanes.start
        out_ref[:, lanes] = (pending.pop(tile)[:, :count] * gain_ref[:, lanes]).astype(jnp.bfloat16)

    for tile, offset, span in windows(width):
        lanes = slice(tile * LANES, tile * LANES + span)
        steps = pl.cdiv(span, LANES)
        block = jnp.concatenate([state_tile(tile + step) for step in range(steps)], axis=1)
        lane = lax.broadcasted_iota(jnp.int32, block.shape, 1)
        block = jnp.where((lane >= offset) & (lane < offset + HD), block, jnp.zeros_like(block))
        pieces = [block]
        if offset:
            pieces.insert(0, jnp.zeros((offset, block.shape[1]), jnp.bfloat16))
        if span - offset - HD:
            pieces.append(jnp.zeros((span - offset - HD, block.shape[1]), jnp.bfloat16))
        right = jnp.concatenate(pieces, axis=0) if len(pieces) > 1 else block
        mixed = jnp.dot(
            jnp.maximum(query_ref[:, lanes], 0), right, preferred_element_type=jnp.float32
        )
        mean_square = jnp.sum(mixed * mixed, axis=1, keepdims=True) * (1.0 / HD)
        normed = mixed * lax.rsqrt(mean_square + epsilon)
        for old in [done for done in pending if done < tile]:
            flush(old)
        for step in range(steps):
            part = normed[:, step * LANES : (step + 1) * LANES]
            at = tile + step
            pending[at] = pending[at] + part if at in pending else part
    for old in sorted(pending):
        flush(old)


def conv_kernel(cur_ref, prev0_ref, prev1_ref, prev2_ref, top_ref, bottom_ref, weight_ref, *rest):
    out_ref, gate_ref = rest[-2:]
    step = pl.program_id(0)
    blocks = pl.num_programs(0)
    block = blocks - 1 - step
    first_gate = FF // BLOCK
    prev_refs = (prev0_ref, prev1_ref, prev2_ref)
    rows = cur_ref.shape[0]

    def conv_tile(lanes):
        weights = weight_ref[:, lanes]
        pick = lambda index: weights[index : index + 1]
        columns = cur_ref.shape[1]
        spread = [
            (
                pick(0) * cur_ref[r, :, lanes].astype(jnp.float32)
                + pick(1) * prev_refs[r][:, lanes].astype(jnp.float32)
            )
            .astype(jnp.bfloat16)
            .astype(jnp.float32)
            for r in range(rows)
        ]
        spread = [top_ref[:, lanes].astype(jnp.float32)] + spread
        spread = spread + [bottom_ref[:, lanes].astype(jnp.float32)]
        column = lax.broadcasted_iota(jnp.int32, (columns, LANES), 0)
        out = []
        for r in range(rows):
            sums = []
            for b in range(3):
                total = pick(2 + b) * spread[r]
                for a in (1, 2):
                    total = total + pick(2 + 3 * a + b) * spread[r + a]
                sums.append(total)
            left = jnp.where(column == 0, 0.0, pltpu.roll(sums[0], 1, 0))
            right = jnp.where(column == columns - 1, 0.0, pltpu.roll(sums[2], columns - 1, 0))
            out.append(pick(11) + sums[1] + left + right)
        return out

    @pl.when(block >= first_gate)
    def _():
        @pl.loop(0, BLOCK // LANES)
        def _(tile):
            lanes = pl.ds(pl.multiple_of(tile * LANES, LANES), LANES)
            base = pl.multiple_of((block - first_gate) * BLOCK + tile * LANES, LANES)
            for r, summed in enumerate(conv_tile(lanes)):
                gate_ref[r, :, pl.ds(base, LANES)] = summed * (1.0 / (1.0 + jnp.exp(-summed)))

    @pl.when(block <= first_gate)
    def _():
        skew = FF % LANES
        start = FF - skew - first_gate * BLOCK

        @pl.loop(0, BLOCK // LANES)
        def _(tile):
            lanes = pl.ds(pl.multiple_of(tile * LANES, LANES), LANES)
            base = pl.multiple_of(block * BLOCK + tile * LANES + start, LANES)
            for r, summed in enumerate(conv_tile(lanes)):
                near = pltpu.roll(gate_ref[r, :, pl.ds(base, LANES)], LANES - skew, 1)
                far = pltpu.roll(gate_ref[r, :, pl.ds(base + LANES, LANES)], LANES - skew, 1)
                lane = lax.broadcasted_iota(jnp.int32, near.shape, 1)
                gate = jnp.where(lane < LANES - skew, near, far)
                out_ref[r, :, lanes] = (summed * gate).astype(jnp.bfloat16)


def conv_frame(hidden, frame, prev, top, bottom, weights, into=None):
    frames, rows, columns, channels = hidden.shape
    blocks = pl.cdiv(channels, BLOCK)
    first_gate = FF // BLOCK
    flat = pl.BlockSpec((pl.Squeezed(), columns, BLOCK), lambda i: (0, 0, blocks - 1 - i))
    specs = [
        pl.BlockSpec(
            (pl.Squeezed(), rows, columns, BLOCK), lambda i: (frame, 0, 0, blocks - 1 - i)
        )
    ]
    if prev is None:
        args = [hidden] * (1 + rows)
        for r in range(rows):
            specs.append(
                pl.BlockSpec(
                    (pl.Squeezed(), pl.Squeezed(), columns, BLOCK),
                    functools.partial(lambda r, i: (frame - 1, r, 0, blocks - 1 - i), r),
                )
            )
    else:
        args = [hidden, *prev]
        specs += [flat] * rows
    args += [top, bottom, weights]
    specs += [flat, flat, pl.BlockSpec((weights.shape[0], BLOCK), lambda i: (0, blocks - 1 - i))]
    aliases = {}
    if into is not None:
        aliases = {len(args): 0}
        args.append(into)
        specs.append(pl.BlockSpec(memory_space=pl.ANY))
    elements = rows * columns * channels
    return pl.pallas_call(
        conv_kernel,
        out_shape=jax.ShapeDtypeStruct((frames, rows, columns, FF), jnp.bfloat16),
        grid=(blocks,),
        in_specs=specs,
        out_specs=pl.BlockSpec(
            (pl.Squeezed(), rows, columns, BLOCK),
            lambda i: (frame, 0, 0, jnp.minimum(blocks - 1 - i, first_gate)),
        ),
        scratch_shapes=[
            pltpu.VMEM((rows, columns, (blocks - first_gate) * BLOCK + LANES), jnp.float32)
        ],
        input_output_aliases=aliases,
        compiler_params=pltpu.CompilerParams(vmem_limit_bytes=32 << 20),
        cost_estimate=pl.CostEstimate(
            flops=elements * 40, bytes_accessed=elements * 6, transcendentals=elements // 2
        ),
        name="conv_frame",
    )(*args)


def whole(body, out_shape, flops, *args):
    specs = [pl.BlockSpec(memory_space=pltpu.SMEM)]
    specs += [pl.BlockSpec(memory_space=pltpu.VMEM)] * (len(args) - 1)
    return pl.pallas_call(
        body,
        out_shape=out_shape,
        in_specs=specs,
        out_specs=pl.BlockSpec(memory_space=pltpu.VMEM),
        compiler_params=pltpu.CompilerParams(vmem_limit_bytes=32 << 20),
        cost_estimate=pl.CostEstimate(flops=flops, bytes_accessed=3 << 20, transcendentals=0),
        name=body.__name__,
    )(*args)


def exchange(value, axis, flip):
    return lax.ppermute(value, axis, [(i, i ^ flip) for i in range(lax.axis_size(axis))])


def ahead(value, axis, steps, wrap=False):
    count = lax.axis_size(axis)
    pairs = [(i, (i + steps) % count) for i in range(count) if wrap or 0 <= i + steps < count]
    return lax.ppermute(value, axis, pairs)


def per_device(
    query_tokens, key_tokens, value_tokens, norm_gain, hidden, time_weight, space_weight, conv_bias
):
    frames, rows, columns, width = query_tokens.shape
    tokens = frames * rows * columns
    channels = hidden.shape[3]
    frame_axes = ("z", "x")
    row = lax.axis_index("row").astype(jnp.int32).reshape(1)
    x = lax.axis_index("x")
    narrow = lambda value: value.astype(jnp.bfloat16)
    wide = lambda value: value.astype(jnp.float32)

    def last_frame_row(r, after=None):
        piece = hidden[frames - 1, r : r + 1]
        if after is not None:
            piece, _ = lax.optimization_barrier((piece, after))
        return ahead(piece, frame_axes, 1)

    def edge(frame, r, before):
        now = wide(hidden[frame, r : r + 1])
        return narrow(time_weight[0] * now + time_weight[1] * wide(before))

    prev_first = last_frame_row(0)

    partial = whole(
        partial_kernel,
        jax.ShapeDtypeStruct((SHARES * SHARE_ROWS, LANES), jnp.bfloat16),
        2 * tokens * width * 256,
        row,
        key_tokens.reshape(tokens, width),
        value_tokens.reshape(tokens, width),
    )
    held = partial.reshape(4, 2, SHARE_ROWS, LANES)
    held = wide(held[:, 0]) + wide(exchange(held[:, 1], "row", 1))
    held = held.reshape(2, 2, SHARE_ROWS, LANES)
    held = held[:, 0] + wide(exchange(narrow(held[:, 1]), "row", 2))
    held = held[0] + wide(exchange(narrow(held[1]), "row", 4))

    sent = narrow(held)
    others = [wide(ahead(sent, "x", k, True)) for k in range(1, INNER)]
    prev_last = last_frame_row(rows - 1, sent)
    prev_middle = last_frame_row(1, sent)
    plane = held + others[0] + others[1] + others[2]
    upto = held
    for k in range(1, INNER):
        upto = upto + jnp.where(x >= k, others[k - 1], 0.0)

    before = jnp.zeros_like(plane)
    for k in (1, 2, 4):
        arrived = wide(ahead(narrow(plane), "z", k))
        plane = plane + arrived
        before = before + arrived
    state = narrow(before + upto)[None]
    state = jnp.stack([state, exchange(state, "row", 4)], axis=1).reshape(2, SHARE_ROWS, LANES)
    state = jnp.stack([state, exchange(state, "row", 2)], axis=1).reshape(4, SHARE_ROWS, LANES)
    state = jnp.stack([state, exchange(state, "row", 1)], axis=1)
    attention = whole(
        mixed_kernel,
        jax.ShapeDtypeStruct((tokens, width), jnp.bfloat16),
        2 * tokens * width * 256,
        row,
        query_tokens.reshape(tokens, width),
        state.reshape(SHARES * SHARE_ROWS, LANES),
        norm_gain[None],
    ).reshape(query_tokens.shape)

    weights = jnp.concatenate(
        [time_weight, space_weight.reshape(9, channels), conv_bias[None]], axis=0
    )
    mine = hidden[frames - 1], hidden[frames - 2]
    up_edge = edge(frames - 1, 0, mine[1][0:1])
    down_edge = edge(frames - 1, rows - 1, mine[1][rows - 1 : rows])
    up_edge, down_edge, _ = lax.optimization_barrier((up_edge, down_edge, sent))
    top, bottom = ahead(down_edge, "row", 1), ahead(up_edge, "row", -1)
    ffn_out = conv_frame(hidden, frames - 1, None, top, bottom, weights)

    bottom = ahead(edge(0, 0, prev_first), "row", -1)
    top = ahead(edge(0, rows - 1, prev_last), "row", 1)
    ffn_out = conv_frame(
        hidden, 0, (prev_first, prev_middle, prev_last), top, bottom, weights, ffn_out
    )
    return (attention, ffn_out)


def solution(mesh):
    frame, row = mesh.shape["frame"], mesh.shape["row"]
    split = Mesh(mesh.devices.reshape(frame // INNER, INNER, row), ("z", "x", "row"))
    tokens = P(("z", "x"), "row", None, None)
    return jax.shard_map(
        per_device,
        mesh=split,
        in_specs=(tokens, tokens, tokens, P(), tokens, P(), P(), P()),
        out_specs=(tokens, tokens),
        check_vma=False,
    )
```

```python
import functools

import jax
import jax.numpy as jnp
from jax import lax
from jax.experimental import pallas as pl
from jax.experimental.pallas import tpu as pltpu
from jax.sharding import Mesh, PartitionSpec as P

HD = 112
FF = 5600
LANES = 128
UNIT = 16
SHARES = 8
SHARE_ROWS = 256
INNER = 4
BLOCK = 11 * LANES
epsilon = 1e-06


def windows(width):
    out = []
    for head in range(width // HD):
        tile, offset = divmod(head * HD, LANES)
        span = LANES if offset + HD <= LANES else 2 * LANES
        out.append((tile, offset, min(span, width - tile * LANES)))
    return out


def unit_row(unit, row):
    share, inside = divmod(unit, UNIT)
    return pl.multiple_of((share ^ row) * SHARE_ROWS + inside * UNIT, UNIT)


def partial_kernel(row_ref, key_ref, value_ref, out_ref):
    row = row_ref[0]
    width = key_ref.shape[1]
    pending = {}

    def flush(tile):
        rounded = pending.pop(tile).astype(jnp.bfloat16)
        for piece in range(HD // UNIT):
            out_ref[pl.ds(unit_row(tile * (HD // UNIT) + piece, row), UNIT), :] = rounded[
                piece * UNIT : (piece + 1) * UNIT
            ]

    for tile, offset, span in windows(width):
        lanes = slice(tile * LANES, tile * LANES + span)
        keys = jnp.maximum(key_ref[:, lanes], 0)
        product = lax.dot_general(
            keys, value_ref[:, lanes], (((0,), (0,)), ((), ())), preferred_element_type=jnp.float32
        )
        block = product[offset : offset + HD]
        lane = lax.broadcasted_iota(jnp.int32, block.shape, 1)
        block = jnp.where((lane >= offset) & (lane < offset + HD), block, 0.0)
        for old in [done for done in pending if done < tile]:
            flush(old)
        for step in range(pl.cdiv(span, LANES)):
            part = block[:, step * LANES : min(span, (step + 1) * LANES)]
            if part.shape[1] < LANES:
                part = jnp.concatenate(
                    [part, jnp.zeros((HD, LANES - part.shape[1]), jnp.float32)], axis=1
                )
            at = tile + step
            pending[at] = pending[at] + part if at in pending else part
    tiles = max(pending) + 1
    for old in sorted(pending):
        flush(old)
    for unit in range(tiles * (HD // UNIT), SHARES * UNIT):
        out_ref[pl.ds(unit_row(unit, row), UNIT), :] = jnp.zeros((UNIT, LANES), jnp.bfloat16)


def mixed_kernel(row_ref, query_ref, state_ref, gain_ref, out_ref):
    row = row_ref[0]
    tokens, width = query_ref.shape
    pending = {}

    def state_tile(tile):
        return jnp.concatenate(
            [
                state_ref[pl.ds(unit_row(tile * (HD // UNIT) + piece, row), UNIT), :]
                for piece in range(HD // UNIT)
            ],
            axis=0,
        )

    def flush(tile):
        lanes = slice(tile * LANES, min(width, (tile + 1) * LANES))
        count = lanes.stop - lanes.start
        out_ref[:, lanes] = (pending.pop(tile)[:, :count] * gain_ref[:, lanes]).astype(jnp.bfloat16)

    for tile, offset, span in windows(width):
        lanes = slice(tile * LANES, tile * LANES + span)
        steps = pl.cdiv(span, LANES)
        block = jnp.concatenate([state_tile(tile + step) for step in range(steps)], axis=1)
        lane = lax.broadcasted_iota(jnp.int32, block.shape, 1)
        block = jnp.where((lane >= offset) & (lane < offset + HD), block, jnp.zeros_like(block))
        pieces = [block]
        if offset:
            pieces.insert(0, jnp.zeros((offset, block.shape[1]), jnp.bfloat16))
        if span - offset - HD:
            pieces.append(jnp.zeros((span - offset - HD, block.shape[1]), jnp.bfloat16))
        right = jnp.concatenate(pieces, axis=0) if len(pieces) > 1 else block
        mixed = jnp.dot(
            jnp.maximum(query_ref[:, lanes], 0), right, preferred_element_type=jnp.float32
        )
        mean_square = jnp.sum(mixed * mixed, axis=1, keepdims=True) * (1.0 / HD)
        normed = mixed * lax.rsqrt(mean_square + epsilon)
        for old in [done for done in pending if done < tile]:
            flush(old)
        for step in range(steps):
            part = normed[:, step * LANES : (step + 1) * LANES]
            at = tile + step
            pending[at] = pending[at] + part if at in pending else part
    for old in sorted(pending):
        flush(old)


def conv_kernel(pieces, cur_ref, *refs):
    count = sum(pieces)
    prev_refs, (top_ref, bottom_ref, weight_ref) = refs[:count], refs[count : count + 3]
    out_ref, gate_ref = refs[-2:]
    block = pl.num_programs(0) - 1 - pl.program_id(0)
    first_gate = FF // BLOCK
    rows, columns, _ = cur_ref.shape
    groups = columns // 8

    def conv_tile(lanes):
        weights = weight_ref[:, lanes]
        pick = [jnp.broadcast_to(weights[i : i + 1], (8, LANES)) for i in range(12)]
        subrow = lax.broadcasted_iota(jnp.int32, (8, LANES), 0)
        first, last = subrow == 0, subrow == 7
        zero = jnp.zeros((8, LANES), jnp.float32)

        def split(value):
            return [value[8 * g : 8 * g + 8] for g in range(value.shape[0] // 8)]

        spread = [split(top_ref[:, lanes].astype(jnp.float32))]
        at = 0
        for r in range(rows):
            now = split(cur_ref[r, :, lanes].astype(jnp.float32))
            old = []
            for ref in prev_refs[at : at + pieces[r]]:
                old += split(ref[:, lanes].astype(jnp.float32))
            at += pieces[r]
            blend = jnp.concatenate([pick[0] * c + pick[1] * p for c, p in zip(now, old)], axis=0)
            spread.append(split(blend.astype(jnp.bfloat16).astype(jnp.float32)))
        spread.append(split(bottom_ref[:, lanes].astype(jnp.float32)))
        out = []
        for r in range(rows):
            sums = []
            for b in range(3):
                sums.append(
                    [
                        pick[2 + b] * spread[r][g]
                        + pick[5 + b] * spread[r + 1][g]
                        + pick[8 + b] * spread[r + 2][g]
                        for g in range(groups)
                    ]
                )
            left = [zero] + [pltpu.roll(value, 1, 0) for value in sums[0]]
            right = [pltpu.roll(value, 7, 0) for value in sums[2]] + [zero]
            out.append(
                [
                    (pick[11] + sums[1][g])
                    + jnp.where(first, left[g], left[g + 1])
                    + jnp.where(last, right[g + 1], right[g])
                    for g in range(groups)
                ]
            )
        return [jnp.concatenate(row, axis=0) for row in out]

    @pl.when(block >= first_gate)
    def _():
        @pl.loop(0, BLOCK // LANES)
        def _(tile):
            lanes = pl.ds(pl.multiple_of(tile * LANES, LANES), LANES)
            base = pl.multiple_of((block - first_gate) * BLOCK + tile * LANES, LANES)
            for r, summed in enumerate(conv_tile(lanes)):
                gate_ref[r, :, pl.ds(base, LANES)] = summed * (1.0 / (1.0 + jnp.exp(-summed)))

    @pl.when(block <= first_gate)
    def _():
        skew = FF % LANES
        start = FF - skew - first_gate * BLOCK

        @pl.loop(0, BLOCK // LANES)
        def _(tile):
            lanes = pl.ds(pl.multiple_of(tile * LANES, LANES), LANES)
            base = pl.multiple_of(block * BLOCK + tile * LANES + start, LANES)
            for r, summed in enumerate(conv_tile(lanes)):
                near = pltpu.roll(gate_ref[r, :, pl.ds(base, LANES)], LANES - skew, 1)
                far = pltpu.roll(gate_ref[r, :, pl.ds(base + LANES, LANES)], LANES - skew, 1)
                lane = lax.broadcasted_iota(jnp.int32, near.shape, 1)
                gate = jnp.where(lane < LANES - skew, near, far)
                out_ref[r, :, lanes] = (summed * gate).astype(jnp.bfloat16)


def conv_frame(hidden, frame, prev, top, bottom, weights, into=None):
    frames, rows, columns, channels = hidden.shape
    blocks = pl.cdiv(channels, BLOCK)
    first_gate = FF // BLOCK
    flat = pl.BlockSpec((pl.Squeezed(), columns, BLOCK), lambda i: (0, 0, blocks - 1 - i))
    specs = [
        pl.BlockSpec(
            (pl.Squeezed(), rows, columns, BLOCK), lambda i: (frame, 0, 0, blocks - 1 - i)
        )
    ]
    args = [hidden]
    if prev is None:
        pieces = (1,) * rows
        for r in range(rows):
            args.append(hidden)
            specs.append(
                pl.BlockSpec(
                    (pl.Squeezed(), pl.Squeezed(), columns, BLOCK),
                    functools.partial(lambda r, i: (frame - 1, r, 0, blocks - 1 - i), r),
                )
            )
    else:
        pieces = tuple(len(row) for row in prev)
        for piece in [piece for row in prev for piece in row]:
            args.append(piece)
            specs.append(
                pl.BlockSpec(
                    (pl.Squeezed(), piece.shape[1], BLOCK), lambda i: (0, 0, blocks - 1 - i)
                )
            )
    args += [top, bottom, weights]
    specs += [flat, flat, pl.BlockSpec((weights.shape[0], BLOCK), lambda i: (0, blocks - 1 - i))]
    aliases = {}
    if into is not None:
        aliases = {len(args): 0}
        args.append(into)
        specs.append(pl.BlockSpec(memory_space=pl.ANY))
    elements = rows * columns * channels
    return pl.pallas_call(
        functools.partial(conv_kernel, pieces),
        out_shape=jax.ShapeDtypeStruct((frames, rows, columns, FF), jnp.bfloat16),
        grid=(blocks,),
        in_specs=specs,
        out_specs=pl.BlockSpec(
            (pl.Squeezed(), rows, columns, BLOCK),
            lambda i: (frame, 0, 0, jnp.minimum(blocks - 1 - i, first_gate)),
        ),
        scratch_shapes=[
            pltpu.VMEM((rows, columns, (blocks - first_gate) * BLOCK + LANES), jnp.float32)
        ],
        input_output_aliases=aliases,
        compiler_params=pltpu.CompilerParams(vmem_limit_bytes=32 << 20),
        cost_estimate=pl.CostEstimate(
            flops=elements * 40, bytes_accessed=elements * 6, transcendentals=elements // 2
        ),
        name="conv_frame",
    )(*args)


def whole(body, out_shape, flops, *args):
    specs = [pl.BlockSpec(memory_space=pltpu.SMEM)]
    specs += [pl.BlockSpec(memory_space=pltpu.VMEM)] * (len(args) - 1)
    return pl.pallas_call(
        body,
        out_shape=out_shape,
        in_specs=specs,
        out_specs=pl.BlockSpec(memory_space=pltpu.VMEM),
        compiler_params=pltpu.CompilerParams(vmem_limit_bytes=32 << 20),
        cost_estimate=pl.CostEstimate(flops=flops, bytes_accessed=3 << 20, transcendentals=0),
        name=body.__name__,
    )(*args)


def exchange(value, axis, flip):
    return lax.ppermute(value, axis, [(i, i ^ flip) for i in range(lax.axis_size(axis))])


def ahead(value, axis, steps, wrap=False):
    count = lax.axis_size(axis)
    pairs = [(i, (i + steps) % count) for i in range(count) if wrap or 0 <= i + steps < count]
    return lax.ppermute(value, axis, pairs)


def behind(value, last):
    planes, inner = lax.axis_size("z"), lax.axis_size("x")
    pairs = []
    for z in range(planes):
        for x in range(inner):
            up = last and x == 1
            if z + up < planes:
                pairs.append((z * inner + x, (z + up) * inner + (x - 1) % inner))
    return lax.ppermute(value, ("z", "x"), pairs)


def per_device(
    query_tokens, key_tokens, value_tokens, norm_gain, hidden, time_weight, space_weight, conv_bias
):
    frames, rows, columns, width = query_tokens.shape
    tokens = frames * rows * columns
    channels = hidden.shape[3]
    frame_axes = ("z", "x")
    row = lax.axis_index("row").astype(jnp.int32).reshape(1)
    x = lax.axis_index("x")
    narrow = lambda value: value.astype(jnp.bfloat16)
    wide = lambda value: value.astype(jnp.float32)

    def tie(value, *others):
        return lax.optimization_barrier((value, *others))[0]

    def last_frame(r, start, stop, after=None):
        source = hidden if after is None else tie(hidden, after)
        return source[frames - 1, r : r + 1, start:stop]

    def edge(source, frame, r, before, part=slice(None)):
        now = wide(source[frame, r : r + 1, part])
        return narrow(time_weight[0] * now + time_weight[1] * wide(before))

    cut = columns // 16 * 8 + 8
    first_a = ahead(last_frame(0, 0, cut), frame_axes, 1)

    partial = whole(
        partial_kernel,
        jax.ShapeDtypeStruct((SHARES * SHARE_ROWS, LANES), jnp.bfloat16),
        2 * tokens * width * 256,
        row,
        key_tokens.reshape(tokens, width),
        value_tokens.reshape(tokens, width),
    )
    first_b = ahead(last_frame(0, cut, columns, partial), frame_axes, 1)
    prev_last = ahead(last_frame(rows - 1, 0, columns, partial), frame_axes, 1)
    middle_a = behind(last_frame(1, 0, cut, partial), False)
    held = partial.reshape(4, 2, SHARE_ROWS, LANES)
    held = wide(held[:, 0]) + wide(exchange(held[:, 1], "row", 1))
    held = held.reshape(2, 2, SHARE_ROWS, LANES)
    held = held[:, 0] + wide(exchange(narrow(held[:, 1]), "row", 2))
    held = held[0] + wide(exchange(narrow(held[1]), "row", 4))

    later = tie(hidden, held)
    up_edge = edge(later, frames - 1, 0, later[frames - 2, 0:1])
    down_edge = edge(later, frames - 1, rows - 1, later[frames - 2, rows - 1 : rows])
    mine = ahead(down_edge, "row", 1), ahead(up_edge, "row", -1)

    weights = jnp.concatenate(
        [time_weight, space_weight.reshape(9, channels), conv_bias[None]], axis=0
    )

    column = held
    before = jnp.zeros_like(held)
    for k in (1, 2, 4):
        sent = narrow(column)
        if k == 1:
            sent, first_a, middle_a = lax.optimization_barrier((sent, first_a, middle_a))
            middle_a = behind(middle_a, False)
        if k == 2:
            sent, first_b = lax.optimization_barrier((sent, first_b))
            up_edge = [
                edge(hidden, 0, 0, first_a, slice(0, cut)),
                edge(hidden, 0, 0, first_b, slice(cut, columns)),
            ]
            bottom = ahead(jnp.concatenate(up_edge, axis=1), "row", -1)
        if k == 4:
            sent, mine, middle_a = lax.optimization_barrier((sent, mine, middle_a))
            ffn_out = conv_frame(hidden, frames - 1, None, *mine, weights)
            middle_a = behind(middle_a, True)
        arrived = wide(ahead(sent, "z", k))
        column = column + arrived
        before = before + arrived
    closed, opened, prev_last, middle_a, ffn_out, bottom = lax.optimization_barrier(
        (narrow(column), narrow(before), prev_last, middle_a, ffn_out, bottom)
    )
    top = ahead(edge(hidden, 0, rows - 1, prev_last), "row", 1)
    prefix = column
    for k in range(1, INNER):
        sent = jnp.where(x + k < INNER, closed, opened)
        prefix = prefix + wide(ahead(sent, "x", k, True))
    middle_b = ahead(last_frame(1, cut, columns, prefix), frame_axes, 1)

    state = narrow(prefix)[None]
    state = jnp.stack([state, exchange(state, "row", 4)], axis=1).reshape(2, SHARE_ROWS, LANES)
    state = jnp.stack([state, exchange(state, "row", 2)], axis=1).reshape(4, SHARE_ROWS, LANES)
    state, middle_b, top = lax.optimization_barrier((state, middle_b, top))
    state = jnp.stack([state, exchange(state, "row", 1)], axis=1)
    attention = whole(
        mixed_kernel,
        jax.ShapeDtypeStruct((tokens, width), jnp.bfloat16),
        2 * tokens * width * 256,
        row,
        query_tokens.reshape(tokens, width),
        state.reshape(SHARES * SHARE_ROWS, LANES),
        norm_gain[None],
    ).reshape(query_tokens.shape)
    ffn_out = conv_frame(
        hidden,
        0,
        ((first_a, first_b), (middle_a, middle_b), (prev_last,)),
        top,
        bottom,
        weights,
        ffn_out,
    )
    return (attention, ffn_out)


def solution(mesh):
    frame, row = mesh.shape["frame"], mesh.shape["row"]
    split = Mesh(mesh.devices.reshape(frame // INNER, INNER, row), ("z", "x", "row"))
    tokens = P(("z", "x"), "row", None, None)
    return jax.shard_map(
        per_device,
        mesh=split,
        in_specs=(tokens, tokens, tokens, P(), tokens, P(), P(), P()),
        out_specs=(tokens, tokens),
        check_vma=False,
    )
```

```python
import functools

import jax
import jax.numpy as jnp
from jax import lax
from jax.experimental import pallas as pl
from jax.experimental.pallas import tpu as pltpu
from jax.sharding import Mesh, PartitionSpec as P

HD = 112
FF = 5600
LANES = 128
UNIT = 16
SHARES = 8
SHARE_ROWS = 256
INNER = 4
BLOCK = 11 * LANES
epsilon = 1e-06


def windows(width):
    out = []
    for head in range(width // HD):
        tile, offset = divmod(head * HD, LANES)
        span = LANES if offset + HD <= LANES else 2 * LANES
        out.append((tile, offset, min(span, width - tile * LANES)))
    return out


def unit_row(unit, row):
    share, inside = divmod(unit, UNIT)
    return pl.multiple_of((share ^ row) * SHARE_ROWS + inside * UNIT, UNIT)


def partial_kernel(row_ref, key_ref, value_ref, token_ref, out_ref):
    row = row_ref[0]
    width = key_ref.shape[1]
    pending = {}

    def flush(tile):
        rounded = pending.pop(tile).astype(jnp.bfloat16)
        for piece in range(HD // UNIT):
            out_ref[pl.ds(unit_row(tile * (HD // UNIT) + piece, row), UNIT), :] = rounded[
                piece * UNIT : (piece + 1) * UNIT
            ]

    for tile, offset, span in windows(width):
        lanes = slice(tile * LANES, tile * LANES + span)
        keys = jnp.maximum(key_ref[:, lanes], 0)
        product = lax.dot_general(
            keys, value_ref[:, lanes], (((0,), (0,)), ((), ())), preferred_element_type=jnp.float32
        )
        block = product[offset : offset + HD]
        lane = lax.broadcasted_iota(jnp.int32, block.shape, 1)
        block = jnp.where((lane >= offset) & (lane < offset + HD), block, 0.0)
        for old in [done for done in pending if done < tile]:
            flush(old)
        for step in range(pl.cdiv(span, LANES)):
            part = block[:, step * LANES : min(span, (step + 1) * LANES)]
            if part.shape[1] < LANES:
                part = jnp.concatenate(
                    [part, jnp.zeros((HD, LANES - part.shape[1]), jnp.float32)], axis=1
                )
            at = tile + step
            pending[at] = pending[at] + part if at in pending else part
    tiles = max(pending) + 1
    for old in sorted(pending):
        flush(old)
    for unit in range(tiles * (HD // UNIT), SHARES * UNIT):
        out_ref[pl.ds(unit_row(unit, row), UNIT), :] = jnp.zeros((UNIT, LANES), jnp.bfloat16)


def mixed_kernel(row_ref, query_ref, state_ref, gain_ref, out_ref):
    row = row_ref[0]
    tokens, width = query_ref.shape
    pending = {}

    def state_tile(tile):
        return jnp.concatenate(
            [
                state_ref[pl.ds(unit_row(tile * (HD // UNIT) + piece, row), UNIT), :]
                for piece in range(HD // UNIT)
            ],
            axis=0,
        )

    def flush(tile):
        lanes = slice(tile * LANES, min(width, (tile + 1) * LANES))
        count = lanes.stop - lanes.start
        out_ref[:, lanes] = (pending.pop(tile)[:, :count] * gain_ref[:, lanes]).astype(jnp.bfloat16)

    for tile, offset, span in windows(width):
        lanes = slice(tile * LANES, tile * LANES + span)
        steps = pl.cdiv(span, LANES)
        block = jnp.concatenate([state_tile(tile + step) for step in range(steps)], axis=1)
        lane = lax.broadcasted_iota(jnp.int32, block.shape, 1)
        block = jnp.where((lane >= offset) & (lane < offset + HD), block, jnp.zeros_like(block))
        pieces = [block]
        if offset:
            pieces.insert(0, jnp.zeros((offset, block.shape[1]), jnp.bfloat16))
        if span - offset - HD:
            pieces.append(jnp.zeros((span - offset - HD, block.shape[1]), jnp.bfloat16))
        right = jnp.concatenate(pieces, axis=0) if len(pieces) > 1 else block
        mixed = jnp.dot(
            jnp.maximum(query_ref[:, lanes], 0), right, preferred_element_type=jnp.float32
        )
        mean_square = jnp.sum(mixed * mixed, axis=1, keepdims=True) * (1.0 / HD)
        normed = mixed * lax.rsqrt(mean_square + epsilon)
        for old in [done for done in pending if done < tile]:
            flush(old)
        for step in range(steps):
            part = normed[:, step * LANES : (step + 1) * LANES]
            at = tile + step
            pending[at] = pending[at] + part if at in pending else part
    for old in sorted(pending):
        flush(old)


def conv_kernel(pieces, cur_ref, *refs):
    count = sum(pieces)
    prev_refs, (top_ref, bottom_ref) = refs[:count], refs[count : count + 2]
    time_ref, space_ref, bias_ref = refs[count + 2 : count + 5]
    out_ref, gate_ref = refs[-2:]
    block = pl.num_programs(0) - 1 - pl.program_id(0)
    first_gate = FF // BLOCK
    rows, columns, _ = cur_ref.shape
    groups = columns // 8

    def conv_tile(lanes):
        times, bias = time_ref[:, lanes], bias_ref[:, lanes]
        lines = [times[0:1], times[1:2]]
        for a in range(3):
            taps = space_ref[a, :, lanes]
            lines += [taps[b : b + 1] for b in range(3)]
        lines.append(bias)
        pick = [jnp.broadcast_to(line, (8, LANES)) for line in lines]
        subrow = lax.broadcasted_iota(jnp.int32, (8, LANES), 0)
        first, last = subrow == 0, subrow == 7
        zero = jnp.zeros((8, LANES), jnp.float32)

        def split(value):
            return [value[8 * g : 8 * g + 8] for g in range(value.shape[0] // 8)]

        spread = [split(top_ref[:, lanes].astype(jnp.float32))]
        at = 0
        for r in range(rows):
            now = split(cur_ref[r, :, lanes].astype(jnp.float32))
            old = []
            for ref in prev_refs[at : at + pieces[r]]:
                old += split(ref[:, lanes].astype(jnp.float32))
            at += pieces[r]
            blend = jnp.concatenate([pick[0] * c + pick[1] * p for c, p in zip(now, old)], axis=0)
            spread.append(split(blend.astype(jnp.bfloat16).astype(jnp.float32)))
        spread.append(split(bottom_ref[:, lanes].astype(jnp.float32)))
        out = []
        for r in range(rows):
            sums = []
            for b in range(3):
                sums.append(
                    [
                        pick[2 + b] * spread[r][g]
                        + pick[5 + b] * spread[r + 1][g]
                        + pick[8 + b] * spread[r + 2][g]
                        for g in range(groups)
                    ]
                )
            left = [zero] + [pltpu.roll(value, 1, 0) for value in sums[0]]
            right = [pltpu.roll(value, 7, 0) for value in sums[2]] + [zero]
            out.append(
                [
                    (pick[11] + sums[1][g])
                    + jnp.where(first, left[g], left[g + 1])
                    + jnp.where(last, right[g + 1], right[g])
                    for g in range(groups)
                ]
            )
        return [jnp.concatenate(row, axis=0) for row in out]

    @pl.when(block >= first_gate)
    def _():
        @pl.loop(0, BLOCK // LANES)
        def _(tile):
            lanes = pl.ds(pl.multiple_of(tile * LANES, LANES), LANES)
            base = pl.multiple_of((block - first_gate) * BLOCK + tile * LANES, LANES)
            for r, summed in enumerate(conv_tile(lanes)):
                gate_ref[r, :, pl.ds(base, LANES)] = summed * (1.0 / (1.0 + jnp.exp(-summed)))

    @pl.when(block <= first_gate)
    def _():
        skew = FF % LANES
        start = FF - skew - first_gate * BLOCK

        @pl.loop(0, BLOCK // LANES)
        def _(tile):
            lanes = pl.ds(pl.multiple_of(tile * LANES, LANES), LANES)
            base = pl.multiple_of(block * BLOCK + tile * LANES + start, LANES)
            for r, summed in enumerate(conv_tile(lanes)):
                near = pltpu.roll(gate_ref[r, :, pl.ds(base, LANES)], LANES - skew, 1)
                far = pltpu.roll(gate_ref[r, :, pl.ds(base + LANES, LANES)], LANES - skew, 1)
                lane = lax.broadcasted_iota(jnp.int32, near.shape, 1)
                gate = jnp.where(lane < LANES - skew, near, far)
                out_ref[r, :, lanes] = (summed * gate).astype(jnp.bfloat16)


def conv_frame(hidden, frame, prev, top, bottom, weights, into=None):
    frames, rows, columns, channels = hidden.shape
    blocks = pl.cdiv(channels, BLOCK)
    first_gate = FF // BLOCK
    flat = pl.BlockSpec((pl.Squeezed(), columns, BLOCK), lambda i: (0, 0, blocks - 1 - i))
    specs = [
        pl.BlockSpec(
            (pl.Squeezed(), rows, columns, BLOCK), lambda i: (frame, 0, 0, blocks - 1 - i)
        )
    ]
    args = [hidden]
    if prev is None:
        pieces = (1,) * rows
        for r in range(rows):
            args.append(hidden)
            specs.append(
                pl.BlockSpec(
                    (pl.Squeezed(), pl.Squeezed(), columns, BLOCK),
                    functools.partial(lambda r, i: (frame - 1, r, 0, blocks - 1 - i), r),
                )
            )
    else:
        ends, middle = prev
        pieces = (1,) * rows
        args += [ends, middle, ends]
        for at in (0, 0, 1):
            specs.append(
                pl.BlockSpec(
                    (pl.Squeezed(), columns, BLOCK),
                    functools.partial(lambda at, i: (at, 0, blocks - 1 - i), at),
                )
            )
    args += [top, bottom, *weights]
    specs += [
        flat,
        flat,
        pl.BlockSpec((2, BLOCK), lambda i: (0, blocks - 1 - i)),
        pl.BlockSpec((3, 3, BLOCK), lambda i: (0, 0, blocks - 1 - i)),
        pl.BlockSpec((1, BLOCK), lambda i: (0, blocks - 1 - i)),
    ]
    aliases = {}
    if into is not None:
        aliases = {len(args): 0}
        args.append(into)
        specs.append(pl.BlockSpec(memory_space=pl.ANY))
    elements = rows * columns * channels
    return pl.pallas_call(
        functools.partial(conv_kernel, pieces),
        out_shape=jax.ShapeDtypeStruct((frames, rows, columns, FF), jnp.bfloat16),
        grid=(blocks,),
        in_specs=specs,
        out_specs=pl.BlockSpec(
            (pl.Squeezed(), rows, columns, BLOCK),
            lambda i: (frame, 0, 0, jnp.minimum(blocks - 1 - i, first_gate)),
        ),
        scratch_shapes=[
            pltpu.VMEM((rows, columns, (blocks - first_gate) * BLOCK + LANES), jnp.float32)
        ],
        input_output_aliases=aliases,
        compiler_params=pltpu.CompilerParams(vmem_limit_bytes=14 << 20),
        cost_estimate=pl.CostEstimate(
            flops=elements * 40, bytes_accessed=elements * 6, transcendentals=elements // 2
        ),
        name="conv_frame",
    )(*kept(args))


def edge_kernel(now0_ref, now2_ref, old0_ref, old2_ref, time_ref, *refs):
    up_ref, down_ref, token_ref = refs[-3:]
    token_ref[...] = jnp.zeros_like(token_ref)
    for now_ref, old_ref, out_ref in ((now0_ref, old0_ref, up_ref), (now2_ref, old2_ref, down_ref)):
        now, old = now_ref[...].astype(jnp.float32), old_ref[...].astype(jnp.float32)
        out_ref[...] = (time_ref[0:1] * now + time_ref[1:2] * old).astype(jnp.bfloat16)
    if len(refs) > 3:
        now1_ref, ends_ref, middle_ref = refs[:3]
        ends_ref[0] = now0_ref[...]
        ends_ref[1] = now2_ref[...]
        middle_ref[...] = now1_ref[...]


def edges(hidden, frame, old, times):
    frames, rows, columns, channels = hidden.shape
    size = 2 * BLOCK

    def take(at, r):
        return pl.BlockSpec(
            (pl.Squeezed(), pl.Squeezed(), columns, size), lambda i: (at, r, 0, i)
        )

    flat = pl.BlockSpec((pl.Squeezed(), columns, size), lambda i: (0, 0, i))
    line = jax.ShapeDtypeStruct((1, columns, channels), jnp.bfloat16)
    args, specs = [hidden, hidden], [take(frame, 0), take(frame, rows - 1)]
    if old is None:
        args += [hidden, hidden]
        specs += [take(frame - 1, 0), take(frame - 1, rows - 1)]
    else:
        args += [old, old]
        specs += [flat, pl.BlockSpec((pl.Squeezed(), columns, size), lambda i: (1, 0, i))]
    args.append(times)
    specs.append(pl.BlockSpec((2, size), lambda i: (0, i)))
    out_shape = [line, line, jax.ShapeDtypeStruct((8, LANES), jnp.float32)]
    out_specs = [flat, flat, pl.BlockSpec((8, LANES), lambda i: (0, 0))]
    if old is None:
        args.append(hidden)
        specs.append(take(frame, 1))
        both = jax.ShapeDtypeStruct((2, columns, channels), jnp.bfloat16)
        out_shape = [both, line] + out_shape
        out_specs = [pl.BlockSpec((2, columns, size), lambda i: (0, 0, i)), flat] + out_specs
    return pl.pallas_call(
        edge_kernel,
        out_shape=out_shape,
        grid=(pl.cdiv(channels, size),),
        in_specs=specs,
        out_specs=out_specs,
        compiler_params=pltpu.CompilerParams(vmem_limit_bytes=14 << 20),
        cost_estimate=pl.CostEstimate(
            flops=6 * columns * channels, bytes_accessed=12 * columns * channels, transcendentals=0
        ),
        name="edges",
    )(*kept(args))


def kept(args):
    return [
        pltpu.with_memory_space_constraint(arg, pltpu.HBM) if arg.ndim == 4 else arg for arg in args
    ]


def whole(body, out_shape, flops, *args):
    specs = [pl.BlockSpec(memory_space=pltpu.SMEM)]
    specs += [pl.BlockSpec(memory_space=pltpu.VMEM)] * (len(args) - 1)
    return pl.pallas_call(
        body,
        out_shape=out_shape,
        in_specs=specs,
        out_specs=pl.BlockSpec(memory_space=pltpu.VMEM),
        compiler_params=pltpu.CompilerParams(vmem_limit_bytes=14 << 20),
        cost_estimate=pl.CostEstimate(flops=flops, bytes_accessed=3 << 20, transcendentals=0),
        name=body.__name__,
    )(*args)


def exchange(value, axis, flip):
    return lax.ppermute(value, axis, [(i, i ^ flip) for i in range(lax.axis_size(axis))])


def ahead(value, axis, steps, wrap=False):
    count = lax.axis_size(axis)
    pairs = [(i, (i + steps) % count) for i in range(count) if wrap or 0 <= i + steps < count]
    return lax.ppermute(value, axis, pairs)


def per_device(
    query_tokens, key_tokens, value_tokens, norm_gain, hidden, time_weight, space_weight, conv_bias
):
    frames, rows, columns, width = query_tokens.shape
    tokens = frames * rows * columns
    channels = hidden.shape[3]
    frame_axes = ("z", "x")
    row = lax.axis_index("row").astype(jnp.int32).reshape(1)
    x = lax.axis_index("x")
    narrow = lambda value: value.astype(jnp.bfloat16)
    wide = lambda value: value.astype(jnp.float32)

    def tie(value, *others):
        return lax.optimization_barrier((value, *others))[0]

    weights = time_weight, space_weight, conv_bias[None]
    ends, middle, up_edge, down_edge, token = edges(hidden, frames - 1, None, time_weight)
    ends = ahead(ends, frame_axes, 1)
    partial = whole(
        partial_kernel,
        jax.ShapeDtypeStruct((SHARES * SHARE_ROWS, LANES), jnp.bfloat16),
        2 * tokens * width * 256,
        row,
        key_tokens.reshape(tokens, width),
        value_tokens.reshape(tokens, width),
        token,
    )
    held = partial.reshape(4, 2, SHARE_ROWS, LANES)
    held = wide(held[:, 0]) + wide(exchange(held[:, 1], "row", 1))
    held = held.reshape(2, 2, SHARE_ROWS, LANES)
    held = held[:, 0] + wide(exchange(narrow(held[:, 1]), "row", 2))
    held = held[0] + wide(exchange(narrow(held[1]), "row", 4))

    up_edge, down_edge = lax.optimization_barrier((up_edge, down_edge, held))[:2]
    top, bottom = ahead(down_edge, "row", 1), ahead(up_edge, "row", -1)

    column = held
    before = jnp.zeros_like(held)
    for k in (1, 2, 4):
        sent = narrow(column)
        if k == 4:
            ffn_out = conv_frame(hidden, frames - 1, None, top, bottom, weights)
        arrived = ahead(sent, "z", k)
        if k == 4:
            arrived, ffn_out = lax.optimization_barrier((arrived, ffn_out))
        arrived = wide(arrived)
        column = column + arrived
        before = before + arrived
    closed, opened = lax.optimization_barrier((narrow(column), narrow(before), ends))[:2]
    up_edge, down_edge, _ = edges(hidden, 0, ends, time_weight)
    prefix = column
    for k in range(1, INNER):
        sent = jnp.where(x + k < INNER, closed, opened)
        prefix = prefix + wide(ahead(sent, "x", k, True))
    middle = ahead(tie(middle, prefix), frame_axes, 1)
    top, bottom = ahead(down_edge, "row", 1), ahead(up_edge, "row", -1)

    state = narrow(prefix)[None]
    state = jnp.stack([state, exchange(state, "row", 4)], axis=1).reshape(2, SHARE_ROWS, LANES)
    state = jnp.stack([state, exchange(state, "row", 2)], axis=1).reshape(4, SHARE_ROWS, LANES)
    state = jnp.stack([state, exchange(state, "row", 1)], axis=1)
    attention = whole(
        mixed_kernel,
        jax.ShapeDtypeStruct((tokens, width), jnp.bfloat16),
        2 * tokens * width * 256,
        row,
        query_tokens.reshape(tokens, width),
        state.reshape(SHARES * SHARE_ROWS, LANES),
        norm_gain[None],
    )
    ffn_out = conv_frame(hidden, 0, (ends, middle), top, bottom, weights, ffn_out)
    return (attention.reshape(query_tokens.shape), ffn_out)


def solution(mesh):
    frame, row = mesh.shape["frame"], mesh.shape["row"]
    split = Mesh(mesh.devices.reshape(frame // INNER, INNER, row), ("z", "x", "row"))
    tokens = P(("z", "x"), "row", None, None)
    return jax.shard_map(
        per_device,
        mesh=split,
        in_specs=(tokens, tokens, tokens, P(), tokens, P(), P(), P()),
        out_specs=(tokens, tokens),
        check_vma=False,
    )
```

```python
import functools

import jax
import jax.numpy as jnp
from jax import lax
from jax.experimental import pallas as pl
from jax.experimental.pallas import tpu as pltpu
from jax.sharding import Mesh, PartitionSpec as P

HD = 112
FF = 5600
LANES = 128
UNIT = 16
SHARES = 8
SHARE_ROWS = 256
INNER = 4
PARTS = 4
epsilon = 1e-06


def windows(width):
    out = []
    for head in range(width // HD):
        tile, offset = divmod(head * HD, LANES)
        span = LANES if offset + HD <= LANES else 2 * LANES
        out.append((tile, offset, min(span, width - tile * LANES)))
    return out


def unit_row(unit, row):
    share, inside = divmod(unit, UNIT)
    place = share ^ row
    place = ((place & 1) << 2) | (place & 2) | (place >> 2)
    return pl.multiple_of(place * SHARE_ROWS + inside * UNIT, UNIT)


def partial_kernel(row_ref, key_ref, value_ref, token_ref, out_ref):
    row = row_ref[0]
    width = key_ref.shape[1]
    pending = {}

    def flush(tile):
        rounded = pending.pop(tile).astype(jnp.bfloat16)
        for piece in range(HD // UNIT):
            out_ref[pl.ds(unit_row(tile * (HD // UNIT) + piece, row), UNIT), :] = rounded[
                piece * UNIT : (piece + 1) * UNIT
            ]

    for tile, offset, span in windows(width):
        lanes = slice(tile * LANES, tile * LANES + span)
        keys = jnp.maximum(key_ref[:, lanes], 0)
        product = lax.dot_general(
            keys, value_ref[:, lanes], (((0,), (0,)), ((), ())), preferred_element_type=jnp.float32
        )
        block = product[offset : offset + HD]
        lane = lax.broadcasted_iota(jnp.int32, block.shape, 1)
        block = jnp.where((lane >= offset) & (lane < offset + HD), block, 0.0)
        for old in [done for done in pending if done < tile]:
            flush(old)
        for step in range(pl.cdiv(span, LANES)):
            part = block[:, step * LANES : min(span, (step + 1) * LANES)]
            if part.shape[1] < LANES:
                part = jnp.concatenate(
                    [part, jnp.zeros((HD, LANES - part.shape[1]), jnp.float32)], axis=1
                )
            at = tile + step
            pending[at] = pending[at] + part if at in pending else part
    tiles = max(pending) + 1
    for old in sorted(pending):
        flush(old)
    for unit in range(tiles * (HD // UNIT), SHARES * UNIT):
        out_ref[pl.ds(unit_row(unit, row), UNIT), :] = jnp.zeros((UNIT, LANES), jnp.bfloat16)


def mixed_kernel(row_ref, query_ref, state_ref, gain_ref, out_ref):
    row = row_ref[0]
    tokens, width = query_ref.shape
    pending = {}

    def state_tile(tile):
        return jnp.concatenate(
            [
                state_ref[pl.ds(unit_row(tile * (HD // UNIT) + piece, row), UNIT), :]
                for piece in range(HD // UNIT)
            ],
            axis=0,
        )

    def flush(tile):
        lanes = slice(tile * LANES, min(width, (tile + 1) * LANES))
        count = lanes.stop - lanes.start
        out_ref[:, lanes] = (pending.pop(tile)[:, :count] * gain_ref[:, lanes]).astype(jnp.bfloat16)

    for tile, offset, span in windows(width):
        lanes = slice(tile * LANES, tile * LANES + span)
        steps = pl.cdiv(span, LANES)
        block = jnp.concatenate([state_tile(tile + step) for step in range(steps)], axis=1)
        lane = lax.broadcasted_iota(jnp.int32, block.shape, 1)
        block = jnp.where((lane >= offset) & (lane < offset + HD), block, jnp.zeros_like(block))
        pieces = [block]
        if offset:
            pieces.insert(0, jnp.zeros((offset, block.shape[1]), jnp.bfloat16))
        if span - offset - HD:
            pieces.append(jnp.zeros((span - offset - HD, block.shape[1]), jnp.bfloat16))
        right = jnp.concatenate(pieces, axis=0) if len(pieces) > 1 else block
        mixed = jnp.dot(
            jnp.maximum(query_ref[:, lanes], 0), right, preferred_element_type=jnp.float32
        )
        mean_square = jnp.sum(mixed * mixed, axis=1, keepdims=True) * (1.0 / HD)
        normed = mixed * lax.rsqrt(mean_square + epsilon)
        for old in [done for done in pending if done < tile]:
            flush(old)
        for step in range(steps):
            part = normed[:, step * LANES : (step + 1) * LANES]
            at = tile + step
            pending[at] = pending[at] + part if at in pending else part
    for old in sorted(pending):
        flush(old)


def conv_kernel(frame, own_ref, *refs):
    *_, out_ref, held_ref, done_ref, sems, held_sems = refs
    if frame:
        prev_refs = [held_ref.at[0, r] for r in range(own_ref.shape[1])]
    else:
        prev_refs, refs = [ref.at[0] for ref in refs[:3]], refs[3:]
    top_ref, bottom_ref, time_ref, space_ref, bias_ref = refs[:5]
    cur_ref = held_ref.at[-1 % held_ref.shape[0]]
    rows, columns, channels = cur_ref.shape
    groups = columns // 8
    skew = FF % LANES
    lead = FF // LANES
    bounds = [lead * part // PARTS for part in range(PARTS + 1)]
    fetches = []
    for part, (start, stop) in enumerate(zip(bounds, bounds[1:])):
        gate_start = lead + start + (part > 0)
        gate_stop = min(channels, (lead + stop + 1) * LANES) if part < PARTS - 1 else channels
        spans = (start * LANES, stop * LANES), (gate_start * LANES, gate_stop)
        fetches.append(
            [
                pltpu.make_async_copy(
                    own_ref.at[pl.ds(0, held_ref.shape[0]), :, :, pl.ds(a, b - a)],
                    held_ref.at[:, :, :, pl.ds(a, b - a)],
                    held_sems.at[part, which],
                )
                for which, (a, b) in enumerate(spans)
            ]
        )
        for fetch in fetches[-1]:
            fetch.start()

    def conv_tile(lanes):
        times = time_ref[:, lanes]
        lines = [times[0:1], times[1:2]]
        for a in range(3):
            taps = space_ref[a, :, lanes]
            lines += [taps[b : b + 1] for b in range(3)]
        lines.append(bias_ref[:, lanes])
        shape = (8, lines[0].shape[1])
        pick = [jnp.broadcast_to(line, shape) for line in lines]
        subrow = lax.broadcasted_iota(jnp.int32, shape, 0)
        first, last = subrow == 0, subrow == 7
        zero = jnp.zeros(shape, jnp.float32)

        def split(value):
            return [value[8 * g : 8 * g + 8] for g in range(groups)]

        spread = [split(top_ref[0, :, lanes].astype(jnp.float32))]
        for r in range(rows):
            now = split(cur_ref[r, :, lanes].astype(jnp.float32))
            old = split(prev_refs[r][:, lanes].astype(jnp.float32))
            blend = jnp.concatenate([pick[0] * c + pick[1] * p for c, p in zip(now, old)], axis=0)
            spread.append(split(blend.astype(jnp.bfloat16).astype(jnp.float32)))
        spread.append(split(bottom_ref[0, :, lanes].astype(jnp.float32)))
        out = []
        for r in range(rows):
            sums = []
            for b in range(3):
                sums.append(
                    [
                        pick[2 + b] * spread[r][g]
                        + pick[5 + b] * spread[r + 1][g]
                        + pick[8 + b] * spread[r + 2][g]
                        for g in range(groups)
                    ]
                )
            left = [zero] + [pltpu.roll(value, 1, 0) for value in sums[0]]
            right = [pltpu.roll(value, 7, 0) for value in sums[2]] + [zero]
            out += [
                (pick[11] + sums[1][g])
                + jnp.where(first, left[g], left[g + 1])
                + jnp.where(last, right[g + 1], right[g])
                for g in range(groups)
            ]
        return out

    lane = lax.broadcasted_iota(jnp.int32, (8, LANES), 1)

    def gates(lanes):
        turned = []
        for value in conv_tile(lanes):
            value = value * (1.0 / (1.0 + jnp.exp(-value)))
            if value.shape[1] < LANES:
                rest = jnp.zeros((8, LANES - value.shape[1]), jnp.float32)
                value = jnp.concatenate([value, rest], axis=1)
            turned.append(pltpu.roll(value, LANES - skew, 1))
        return turned

    def step(lanes, near, far, width):
        values = conv_tile(lanes)
        gated = [
            value * jnp.where(lane < LANES - skew, a, b) for value, a, b in zip(values, near, far)
        ]
        for r in range(rows):
            row = jnp.concatenate(gated[r * groups : (r + 1) * groups], axis=0)
            row = row.astype(jnp.bfloat16)
            done_ref[r, :, pl.ds(lanes.start, width)] = row[:, :width]

    def tile_at(index):
        return pl.ds(pl.multiple_of(index * LANES, LANES), LANES)

    def body(tile, near):
        far = gates(tile_at(tile + lead + 1))
        step(tile_at(tile), near, far, LANES)
        return far

    near = None
    for part, (start, stop) in enumerate(zip(bounds, bounds[1:])):
        for fetch in fetches[part]:
            fetch.wait()
        if near is None:
            near = gates(pl.ds(lead * LANES, LANES))
        near = lax.fori_loop(start, stop, body, near)
    last = (lead * 2 + 1) * LANES
    far = gates(pl.ds(last, channels - last))
    step(pl.ds(lead * LANES, LANES), near, far, skew)
    copies = [
        pltpu.make_async_copy(done_ref.at[r], out_ref.at[frame, r], sems.at[r]) for r in range(rows)
    ]
    for copy in copies:
        copy.start()
    for copy in copies:
        copy.wait()


def conv_frame(hidden, frame, prev, top, bottom, weights, into=None):
    frames, rows, columns, channels = hidden.shape
    args = [hidden, *prev, top, bottom, *weights]
    specs = [pl.BlockSpec(memory_space=pltpu.VMEM)] * len(args)
    args[0] = pltpu.with_memory_space_constraint(hidden, pltpu.HBM)
    specs[0] = pl.BlockSpec(memory_space=pl.ANY)
    aliases = {}
    if into is not None:
        aliases = {len(args): 0}
        args.append(into)
        specs.append(pl.BlockSpec(memory_space=pl.ANY))
    elements = rows * columns * channels
    return pl.pallas_call(
        functools.partial(conv_kernel, frame),
        out_shape=jax.ShapeDtypeStruct((frames, rows, columns, FF), jnp.bfloat16),
        in_specs=specs,
        out_specs=pl.BlockSpec(memory_space=pl.ANY),
        scratch_shapes=[
            pltpu.VMEM((frame + 1, rows, columns, channels), jnp.bfloat16),
            pltpu.VMEM((rows, columns, FF), jnp.bfloat16),
            pltpu.SemaphoreType.DMA((rows,)),
            pltpu.SemaphoreType.DMA((PARTS, 2)),
        ],
        input_output_aliases=aliases,
        compiler_params=pltpu.CompilerParams(vmem_limit_bytes=12 << 20),
        cost_estimate=pl.CostEstimate(
            flops=elements * 40, bytes_accessed=elements * 6, transcendentals=elements // 2
        ),
        name="conv_frame",
    )(*args)


def edge_kernel(own_ref, *refs, frame):
    *old_refs, time_ref, _, up_ref, down_ref, now_ref, old_ref, sems = refs
    rows, channels = own_ref.shape[1], own_ref.shape[3]
    ends = (0, rows - 1)
    copies = []
    for at, r in enumerate(ends):
        group = [pltpu.make_async_copy(own_ref.at[frame, r], now_ref.at[at], sems.at[0, at])]
        if frame:
            source = own_ref.at[frame - 1, r]
            group.append(pltpu.make_async_copy(source, old_ref.at[at], sems.at[1, at]))
        copies.append(group)
    for copy in copies[0] + copies[1]:
        copy.start()

    for at, out_ref in enumerate((up_ref, down_ref)):
        old_view = old_ref.at[at] if frame else old_refs[at].at[0]
        for copy in copies[at]:
            copy.wait()

        def blend(lanes):
            times = time_ref[:, lanes]
            now = now_ref[at, :, lanes].astype(jnp.float32)
            old = old_view[:, lanes].astype(jnp.float32)
            out_ref[0, :, lanes] = (times[0:1] * now + times[1:2] * old).astype(jnp.bfloat16)

        wide = 4 * LANES

        @pl.loop(0, channels // wide)
        def _(tile):
            blend(pl.ds(pl.multiple_of(tile * wide, LANES), wide))

        if channels % wide:
            blend(pl.ds(channels // wide * wide, channels % wide))


def edges(hidden, frame, old, times, token):
    channels, columns = hidden.shape[3], hidden.shape[2]
    held = pl.BlockSpec(memory_space=pltpu.VMEM)
    anywhere = pl.BlockSpec(memory_space=pl.ANY)
    args = [pltpu.with_memory_space_constraint(hidden, pltpu.HBM), *old, times, token]
    line = jax.ShapeDtypeStruct((1, columns, channels), jnp.bfloat16)
    pair = pltpu.VMEM((2, columns, channels), jnp.bfloat16)
    return pl.pallas_call(
        functools.partial(edge_kernel, frame=frame),
        out_shape=(line, line),
        in_specs=[anywhere] + [held] * len(old) + [held, anywhere],
        out_specs=(held, held),
        scratch_shapes=[pair, pair, pltpu.SemaphoreType.DMA((2, 2))],
        compiler_params=pltpu.CompilerParams(vmem_limit_bytes=8 << 20),
        cost_estimate=pl.CostEstimate(
            flops=6 * columns * channels, bytes_accessed=12 * columns * channels, transcendentals=0
        ),
        name="edges",
    )(*args)


def copy_kernel(source_ref, *refs, frame, rows):
    *_, token_ref, sems = refs
    outs = refs[-2 - len(rows) : -2]
    copies = [
        pltpu.make_async_copy(source_ref.at[frame, r], out_ref.at[0], sems.at[at])
        for at, (r, out_ref) in enumerate(zip(rows, outs))
    ]
    for copy in copies:
        copy.start()
    token_ref[...] = jnp.zeros_like(token_ref)
    for copy in copies:
        copy.wait()


def copied_rows(hidden, frame, rows, *tokens):
    _, _, columns, channels = hidden.shape
    args = (pltpu.with_memory_space_constraint(hidden, pltpu.HBM), *tokens)
    anywhere = pl.BlockSpec(memory_space=pl.ANY)
    return pl.pallas_call(
        functools.partial(copy_kernel, frame=frame, rows=rows),
        out_shape=[jax.ShapeDtypeStruct((1, columns, channels), jnp.bfloat16) for _ in rows]
        + [jax.ShapeDtypeStruct((8, LANES), jnp.float32)],
        in_specs=[anywhere] * len(args),
        out_specs=[pl.BlockSpec(memory_space=pltpu.VMEM)] * (len(rows) + 1),
        scratch_shapes=[pltpu.SemaphoreType.DMA((len(rows),))],
        cost_estimate=pl.CostEstimate(
            flops=0, bytes_accessed=4 * len(rows) * columns * channels, transcendentals=0
        ),
        name="copied_rows",
    )(*args)


def whole(body, out_shape, flops, *args):
    specs = [pl.BlockSpec(memory_space=pltpu.SMEM)]
    specs += [pl.BlockSpec(memory_space=pltpu.VMEM)] * (len(args) - 1)
    return pl.pallas_call(
        body,
        out_shape=out_shape,
        in_specs=specs,
        out_specs=pl.BlockSpec(memory_space=pltpu.VMEM),
        compiler_params=pltpu.CompilerParams(vmem_limit_bytes=10 << 20),
        cost_estimate=pl.CostEstimate(flops=flops, bytes_accessed=3 << 20, transcendentals=0),
        name=body.__name__,
    )(*args)


def exchange(value, axis, flip):
    return lax.ppermute(value, axis, [(i, i ^ flip) for i in range(lax.axis_size(axis))])


def ahead(value, axis, steps, wrap=False):
    count = lax.axis_size(axis)
    pairs = [(i, (i + steps) % count) for i in range(count) if wrap or 0 <= i + steps < count]
    return lax.ppermute(value, axis, pairs)


def per_device(
    query_tokens, key_tokens, value_tokens, norm_gain, hidden, time_weight, space_weight, conv_bias
):
    frames, rows, columns, width = query_tokens.shape
    tokens = frames * rows * columns
    channels = hidden.shape[3]
    frame_axes = ("z", "x")
    row = lax.axis_index("row").astype(jnp.int32).reshape(1)
    x = lax.axis_index("x")
    narrow = lambda value: value.astype(jnp.bfloat16)
    wide = lambda value: value.astype(jnp.float32)

    weights = time_weight, space_weight, conv_bias[None]
    prev_first, prev_last, token = copied_rows(hidden, frames - 1, (0, rows - 1))
    prev_first, prev_last = ahead(prev_first, frame_axes, 1), ahead(prev_last, frame_axes, 1)
    partial = whole(
        partial_kernel,
        jax.ShapeDtypeStruct((SHARES * SHARE_ROWS, LANES), jnp.bfloat16),
        2 * tokens * width * 256,
        row,
        key_tokens.reshape(tokens, width),
        value_tokens.reshape(tokens, width),
        token,
    )
    held = partial.reshape(2, 4, SHARE_ROWS, LANES)
    held = wide(held[0]) + wide(exchange(held[1], "row", 1))
    held = held[:2] + wide(exchange(narrow(held[2:]), "row", 2))
    held = held[0] + wide(exchange(narrow(held[1]), "row", 4))

    planes = lax.axis_size("z")
    fold = [(z * INNER + INNER - 1, z * INNER + INNER - 2) for z in range(planes)]
    column = held + wide(lax.ppermute(narrow(held), frame_axes, fold))
    before = jnp.zeros_like(held)
    for k in (1, 2, 4):
        sent = narrow(column)
        if k == 2:
            sent, prev_first = lax.optimization_barrier((sent, prev_first))
        if k == 4:
            up_edge, down_edge = edges(hidden, frames - 1, (), time_weight, sent)
            top, bottom = ahead(down_edge, "row", 1), ahead(up_edge, "row", -1)
            ffn_out = conv_frame(hidden, frames - 1, (), top, bottom, weights)
        pairs = [
            (z * INNER + at, (z + k) * INNER + at)
            for z in range(planes - k)
            for at in range(INNER - 1)
        ]
        arrived = lax.ppermute(sent, frame_axes, pairs)
        column = column + wide(arrived)
        before = before + wide(arrived)
    prefix = before + held
    closed, opened = lax.optimization_barrier((narrow(prefix), narrow(before), prev_last))[:2]
    for k in range(1, INNER):
        sent = jnp.where(x + k < INNER, closed, opened)
        prefix = prefix + wide(ahead(sent, "x", k, True))
    prefix = narrow(prefix)
    prev_middle, _ = copied_rows(hidden, frames - 1, (1,), prefix)
    prev_middle = ahead(prev_middle, frame_axes, 1)

    state = jnp.concatenate([prefix, exchange(prefix, "row", 4)], axis=0)
    up_edge, down_edge = edges(hidden, 0, (prev_first, prev_last), time_weight, state)
    top_first, bottom_first = ahead(down_edge, "row", 1), ahead(up_edge, "row", -1)
    state, ffn_out = lax.optimization_barrier((state, ffn_out))
    state = jnp.concatenate([state, exchange(state, "row", 2)], axis=0)
    state, prev_middle = lax.optimization_barrier((state, prev_middle))
    state = jnp.concatenate([state, exchange(state, "row", 1)], axis=0)
    attention = whole(
        mixed_kernel,
        jax.ShapeDtypeStruct((tokens, width), jnp.bfloat16),
        2 * tokens * width * 256,
        row,
        query_tokens.reshape(tokens, width),
        state,
        norm_gain[None],
    )
    ffn_out = conv_frame(
        hidden, 0, (prev_first, prev_middle, prev_last), top_first, bottom_first, weights, ffn_out
    )
    return (attention.reshape(query_tokens.shape), ffn_out)


def solution(mesh):
    frame, row = mesh.shape["frame"], mesh.shape["row"]
    split = Mesh(mesh.devices.reshape(frame // INNER, INNER, row), ("z", "x", "row"))
    tokens = P(("z", "x"), "row", None, None)
    return jax.shard_map(
        per_device,
        mesh=split,
        in_specs=(tokens, tokens, tokens, P(), tokens, P(), P(), P()),
        out_specs=(tokens, tokens),
        check_vma=False,
    )
```

```python
import functools

import jax
import jax.numpy as jnp
from jax import lax
from jax.experimental import pallas as pl
from jax.experimental.pallas import tpu as pltpu
from jax.sharding import Mesh, PartitionSpec as P

HD = 112
FF = 5600
LANES = 128
UNIT = 16
SHARES = 8
SHARE_ROWS = 256
INNER = 4
PARTS = 4
epsilon = 1e-06


def windows(width):
    out = []
    for head in range(width // HD):
        tile, offset = divmod(head * HD, LANES)
        span = LANES if offset + HD <= LANES else 2 * LANES
        out.append((tile, offset, min(span, width - tile * LANES)))
    return out


def unit_row(unit, row):
    share, inside = divmod(unit, UNIT)
    place = share ^ row
    place = ((place & 1) << 2) | (place & 2) | (place >> 2)
    return pl.multiple_of(place * SHARE_ROWS + inside * UNIT, UNIT)


def partial_kernel(row_ref, key_ref, value_ref, token_ref, out_ref):
    row = row_ref[0]
    width = key_ref.shape[1]
    pending = {}

    def flush(tile):
        rounded = pending.pop(tile).astype(jnp.bfloat16)
        for piece in range(HD // UNIT):
            out_ref[pl.ds(unit_row(tile * (HD // UNIT) + piece, row), UNIT), :] = rounded[
                piece * UNIT : (piece + 1) * UNIT
            ]

    for tile, offset, span in windows(width):
        lanes = slice(tile * LANES, tile * LANES + span)
        keys = jnp.maximum(key_ref[:, lanes], 0)
        product = lax.dot_general(
            keys, value_ref[:, lanes], (((0,), (0,)), ((), ())), preferred_element_type=jnp.float32
        )
        block = product[offset : offset + HD]
        lane = lax.broadcasted_iota(jnp.int32, block.shape, 1)
        block = jnp.where((lane >= offset) & (lane < offset + HD), block, 0.0)
        for old in [done for done in pending if done < tile]:
            flush(old)
        for step in range(pl.cdiv(span, LANES)):
            part = block[:, step * LANES : min(span, (step + 1) * LANES)]
            if part.shape[1] < LANES:
                part = jnp.concatenate(
                    [part, jnp.zeros((HD, LANES - part.shape[1]), jnp.float32)], axis=1
                )
            at = tile + step
            pending[at] = pending[at] + part if at in pending else part
    tiles = max(pending) + 1
    for old in sorted(pending):
        flush(old)
    for unit in range(tiles * (HD // UNIT), SHARES * UNIT):
        out_ref[pl.ds(unit_row(unit, row), UNIT), :] = jnp.zeros((UNIT, LANES), jnp.bfloat16)


def mixed_kernel(row_ref, query_ref, state_ref, gain_ref, out_ref):
    row = row_ref[0]
    tokens, width = query_ref.shape
    pending = {}

    def state_tile(tile):
        return jnp.concatenate(
            [
                state_ref[pl.ds(unit_row(tile * (HD // UNIT) + piece, row), UNIT), :]
                for piece in range(HD // UNIT)
            ],
            axis=0,
        )

    def flush(tile):
        lanes = slice(tile * LANES, min(width, (tile + 1) * LANES))
        count = lanes.stop - lanes.start
        out_ref[:, lanes] = (pending.pop(tile)[:, :count] * gain_ref[:, lanes]).astype(jnp.bfloat16)

    for tile, offset, span in windows(width):
        lanes = slice(tile * LANES, tile * LANES + span)
        steps = pl.cdiv(span, LANES)
        block = jnp.concatenate([state_tile(tile + step) for step in range(steps)], axis=1)
        lane = lax.broadcasted_iota(jnp.int32, block.shape, 1)
        block = jnp.where((lane >= offset) & (lane < offset + HD), block, jnp.zeros_like(block))
        pieces = [block]
        if offset:
            pieces.insert(0, jnp.zeros((offset, block.shape[1]), jnp.bfloat16))
        if span - offset - HD:
            pieces.append(jnp.zeros((span - offset - HD, block.shape[1]), jnp.bfloat16))
        right = jnp.concatenate(pieces, axis=0) if len(pieces) > 1 else block
        mixed = jnp.dot(
            jnp.maximum(query_ref[:, lanes], 0), right, preferred_element_type=jnp.float32
        )
        mean_square = jnp.sum(mixed * mixed, axis=1, keepdims=True) * (1.0 / HD)
        normed = mixed * lax.rsqrt(mean_square + epsilon)
        for old in [done for done in pending if done < tile]:
            flush(old)
        for step in range(steps):
            part = normed[:, step * LANES : (step + 1) * LANES]
            at = tile + step
            pending[at] = pending[at] + part if at in pending else part
    for old in sorted(pending):
        flush(old)


def conv_kernel(frame, own_ref, *refs):
    *_, out_ref, held_ref, done_ref, sems, held_sems = refs
    if frame:
        prev_refs = [held_ref.at[0, r] for r in range(own_ref.shape[1])]
    else:
        prev_refs, refs = [ref.at[0] for ref in refs[:3]], refs[3:]
    top_ref, bottom_ref, time_ref, space_ref, bias_ref = refs[:5]
    cur_ref = held_ref.at[-1 % held_ref.shape[0]]
    rows, columns, channels = cur_ref.shape
    groups = columns // 8
    skew = FF % LANES
    lead = FF // LANES
    bounds = [0, lead // 14, lead // 4, lead * 5 // 8, lead]
    fetches = []
    for part, (start, stop) in enumerate(zip(bounds, bounds[1:])):
        gate_start = lead + start + (part > 0)
        gate_stop = min(channels, (lead + stop + 1) * LANES) if part < PARTS - 1 else channels
        spans = (start * LANES, stop * LANES), (gate_start * LANES, gate_stop)
        fetches.append(
            [
                pltpu.make_async_copy(
                    own_ref.at[pl.ds(0, held_ref.shape[0]), :, :, pl.ds(a, b - a)],
                    held_ref.at[:, :, :, pl.ds(a, b - a)],
                    held_sems.at[part, which],
                )
                for which, (a, b) in enumerate(spans)
            ]
        )
        for fetch in fetches[-1]:
            fetch.start()

    def conv_tile(lanes):
        times = time_ref[:, lanes]
        lines = [times[0:1], times[1:2]]
        for a in range(3):
            taps = space_ref[a, :, lanes]
            lines += [taps[b : b + 1] for b in range(3)]
        lines.append(bias_ref[:, lanes])
        shape = (8, lines[0].shape[1])
        pick = [jnp.broadcast_to(line, shape) for line in lines]
        subrow = lax.broadcasted_iota(jnp.int32, shape, 0)
        first, last = subrow == 0, subrow == 7
        zero = jnp.zeros(shape, jnp.float32)

        def split(value):
            return [value[8 * g : 8 * g + 8] for g in range(groups)]

        spread = [split(top_ref[0, :, lanes].astype(jnp.float32))]
        for r in range(rows):
            now = split(cur_ref[r, :, lanes].astype(jnp.float32))
            old = split(prev_refs[r][:, lanes].astype(jnp.float32))
            blend = jnp.concatenate([pick[0] * c + pick[1] * p for c, p in zip(now, old)], axis=0)
            spread.append(split(blend.astype(jnp.bfloat16).astype(jnp.float32)))
        spread.append(split(bottom_ref[0, :, lanes].astype(jnp.float32)))
        out = []
        for r in range(rows):
            sums = []
            for b in range(3):
                sums.append(
                    [
                        pick[2 + b] * spread[r][g]
                        + pick[5 + b] * spread[r + 1][g]
                        + pick[8 + b] * spread[r + 2][g]
                        for g in range(groups)
                    ]
                )
            left = [zero] + [pltpu.roll(value, 1, 0) for value in sums[0]]
            right = [pltpu.roll(value, 7, 0) for value in sums[2]] + [zero]
            out += [
                (pick[11] + sums[1][g])
                + jnp.where(first, left[g], left[g + 1])
                + jnp.where(last, right[g + 1], right[g])
                for g in range(groups)
            ]
        return out

    lane = lax.broadcasted_iota(jnp.int32, (8, LANES), 1)

    def gates(lanes):
        turned = []
        for value in conv_tile(lanes):
            value = value * (1.0 / (1.0 + jnp.exp(-value)))
            if value.shape[1] < LANES:
                rest = jnp.zeros((8, LANES - value.shape[1]), jnp.float32)
                value = jnp.concatenate([value, rest], axis=1)
            turned.append(pltpu.roll(value, LANES - skew, 1))
        return turned

    def step(lanes, near, far, width):
        values = conv_tile(lanes)
        gated = [
            value * jnp.where(lane < LANES - skew, a, b) for value, a, b in zip(values, near, far)
        ]
        for r in range(rows):
            row = jnp.concatenate(gated[r * groups : (r + 1) * groups], axis=0)
            row = row.astype(jnp.bfloat16)
            done_ref[r, :, pl.ds(lanes.start, width)] = row[:, :width]

    def tile_at(index):
        return pl.ds(pl.multiple_of(index * LANES, LANES), LANES)

    def body(tile, near):
        far = gates(tile_at(tile + lead + 1))
        step(tile_at(tile), near, far, LANES)
        return far

    near = None
    for part, (start, stop) in enumerate(zip(bounds, bounds[1:])):
        for fetch in fetches[part]:
            fetch.wait()
        if near is None:
            near = gates(pl.ds(lead * LANES, LANES))
        near = lax.fori_loop(start, stop, body, near)
    last = (lead * 2 + 1) * LANES
    far = gates(pl.ds(last, channels - last))
    step(pl.ds(lead * LANES, LANES), near, far, skew)
    copies = [
        pltpu.make_async_copy(done_ref.at[r], out_ref.at[frame, r], sems.at[r]) for r in range(rows)
    ]
    for copy in copies:
        copy.start()
    for copy in copies:
        copy.wait()


def conv_frame(hidden, frame, prev, top, bottom, weights, into=None):
    frames, rows, columns, channels = hidden.shape
    args = [hidden, *prev, top, bottom, *weights]
    specs = [pl.BlockSpec(memory_space=pltpu.VMEM)] * len(args)
    args[0] = pltpu.with_memory_space_constraint(hidden, pltpu.HBM)
    specs[0] = pl.BlockSpec(memory_space=pl.ANY)
    aliases = {}
    if into is not None:
        aliases = {len(args): 0}
        args.append(into)
        specs.append(pl.BlockSpec(memory_space=pl.ANY))
    elements = rows * columns * channels
    return pl.pallas_call(
        functools.partial(conv_kernel, frame),
        out_shape=jax.ShapeDtypeStruct((frames, rows, columns, FF), jnp.bfloat16),
        in_specs=specs,
        out_specs=pl.BlockSpec(memory_space=pl.ANY),
        scratch_shapes=[
            pltpu.VMEM((frame + 1, rows, columns, channels), jnp.bfloat16),
            pltpu.VMEM((rows, columns, FF), jnp.bfloat16),
            pltpu.SemaphoreType.DMA((rows,)),
            pltpu.SemaphoreType.DMA((PARTS, 2)),
        ],
        input_output_aliases=aliases,
        compiler_params=pltpu.CompilerParams(vmem_limit_bytes=12 << 20),
        cost_estimate=pl.CostEstimate(
            flops=elements * 40, bytes_accessed=elements * 6, transcendentals=elements // 2
        ),
        name="conv_frame",
    )(*args)


def row_copies(source_ref, target_ref, sems):
    return [
        pltpu.make_async_copy(
            source_ref.at[pl.ds(8 * g, 8)], target_ref.at[pl.ds(8 * g, 8)], sems.at[g]
        )
        for g in range(source_ref.shape[0] // 8)
    ]


def edge_kernel(own_ref, *refs, frame):
    *old_refs, time_ref, _, up_ref, down_ref, now_ref, old_ref, sems = refs
    rows, channels = own_ref.shape[1], own_ref.shape[3]
    ends = (0, rows - 1)
    copies = []
    for at, r in enumerate(ends):
        group = row_copies(own_ref.at[frame, r], now_ref.at[at], sems.at[0, at])
        if frame:
            group += row_copies(own_ref.at[frame - 1, r], old_ref.at[at], sems.at[1, at])
        copies.append(group)
    for copy in copies[0] + copies[1]:
        copy.start()

    for at, out_ref in enumerate((up_ref, down_ref)):
        old_view = old_ref.at[at] if frame else old_refs[at].at[0]
        for copy in copies[at]:
            copy.wait()

        def blend(lanes):
            times = time_ref[:, lanes]
            now = now_ref[at, :, lanes].astype(jnp.float32)
            old = old_view[:, lanes].astype(jnp.float32)
            out_ref[0, :, lanes] = (times[0:1] * now + times[1:2] * old).astype(jnp.bfloat16)

        wide = 4 * LANES

        @pl.loop(0, channels // wide)
        def _(tile):
            blend(pl.ds(pl.multiple_of(tile * wide, LANES), wide))

        if channels % wide:
            blend(pl.ds(channels // wide * wide, channels % wide))


def edges(hidden, frame, old, times, token):
    channels, columns = hidden.shape[3], hidden.shape[2]
    held = pl.BlockSpec(memory_space=pltpu.VMEM)
    anywhere = pl.BlockSpec(memory_space=pl.ANY)
    args = [pltpu.with_memory_space_constraint(hidden, pltpu.HBM), *old, times, token]
    line = jax.ShapeDtypeStruct((1, columns, channels), jnp.bfloat16)
    pair = pltpu.VMEM((2, columns, channels), jnp.bfloat16)
    return pl.pallas_call(
        functools.partial(edge_kernel, frame=frame),
        out_shape=(line, line),
        in_specs=[anywhere] + [held] * len(old) + [held, anywhere],
        out_specs=(held, held),
        scratch_shapes=[pair, pair, pltpu.SemaphoreType.DMA((2, 2, columns // 8))],
        compiler_params=pltpu.CompilerParams(vmem_limit_bytes=8 << 20),
        cost_estimate=pl.CostEstimate(
            flops=6 * columns * channels, bytes_accessed=12 * columns * channels, transcendentals=0
        ),
        name="edges",
    )(*args)


def copy_kernel(source_ref, *refs, frame, rows):
    *_, token_ref, sems = refs
    outs = refs[-2 - len(rows) : -2]
    copies = []
    for at, (r, out_ref) in enumerate(zip(rows, outs)):
        copies += row_copies(source_ref.at[frame, r], out_ref.at[0], sems.at[at])
    for copy in copies:
        copy.start()
    token_ref[...] = jnp.zeros_like(token_ref)
    for copy in copies:
        copy.wait()


def copied_rows(hidden, frame, rows, *tokens):
    _, _, columns, channels = hidden.shape
    args = (pltpu.with_memory_space_constraint(hidden, pltpu.HBM), *tokens)
    anywhere = pl.BlockSpec(memory_space=pl.ANY)
    return pl.pallas_call(
        functools.partial(copy_kernel, frame=frame, rows=rows),
        out_shape=[jax.ShapeDtypeStruct((1, columns, channels), jnp.bfloat16) for _ in rows]
        + [jax.ShapeDtypeStruct((8, LANES), jnp.float32)],
        in_specs=[anywhere] * len(args),
        out_specs=[pl.BlockSpec(memory_space=pltpu.VMEM)] * (len(rows) + 1),
        scratch_shapes=[pltpu.SemaphoreType.DMA((len(rows), columns // 8))],
        cost_estimate=pl.CostEstimate(
            flops=0, bytes_accessed=4 * len(rows) * columns * channels, transcendentals=0
        ),
        name="copied_rows",
    )(*args)


def whole(body, out_shape, flops, *args, token=None):
    specs = [pl.BlockSpec(memory_space=pltpu.SMEM)]
    specs += [pl.BlockSpec(memory_space=pltpu.VMEM)] * (len(args) - 1)
    if token is not None:
        args += (token,)
        specs.append(pl.BlockSpec(memory_space=pl.ANY))
    return pl.pallas_call(
        body,
        out_shape=out_shape,
        in_specs=specs,
        out_specs=pl.BlockSpec(memory_space=pltpu.VMEM),
        compiler_params=pltpu.CompilerParams(vmem_limit_bytes=10 << 20),
        cost_estimate=pl.CostEstimate(flops=flops, bytes_accessed=3 << 20, transcendentals=0),
        name=body.__name__,
    )(*args)


def exchange(value, axis, flip):
    return lax.ppermute(value, axis, [(i, i ^ flip) for i in range(lax.axis_size(axis))])


def ahead(value, axis, steps, wrap=False):
    count = lax.axis_size(axis)
    pairs = [(i, (i + steps) % count) for i in range(count) if wrap or 0 <= i + steps < count]
    return lax.ppermute(value, axis, pairs)


def per_device(
    query_tokens, key_tokens, value_tokens, norm_gain, hidden, time_weight, space_weight, conv_bias
):
    frames, rows, columns, width = query_tokens.shape
    tokens = frames * rows * columns
    channels = hidden.shape[3]
    frame_axes = ("z", "x")
    row = lax.axis_index("row").astype(jnp.int32).reshape(1)
    x = lax.axis_index("x")
    narrow = lambda value: value.astype(jnp.bfloat16)
    wide = lambda value: value.astype(jnp.float32)

    weights = time_weight, space_weight, conv_bias[None]
    prev_first, prev_last, token = copied_rows(hidden, frames - 1, (0, rows - 1))
    prev_first, prev_last = ahead(prev_first, frame_axes, 1), ahead(prev_last, frame_axes, 1)
    partial = whole(
        partial_kernel,
        jax.ShapeDtypeStruct((SHARES * SHARE_ROWS, LANES), jnp.bfloat16),
        2 * tokens * width * 256,
        row,
        key_tokens.reshape(tokens, width),
        value_tokens.reshape(tokens, width),
        token=token,
    )
    held = partial.reshape(2, 4, SHARE_ROWS, LANES)
    held = wide(held[0]) + wide(exchange(held[1], "row", 1))
    held = held[:2] + wide(exchange(narrow(held[2:]), "row", 2))
    held = held[0] + wide(exchange(narrow(held[1]), "row", 4))

    planes = lax.axis_size("z")
    fold = [(z * INNER + INNER - 1, z * INNER + INNER - 2) for z in range(planes)]
    column = held + wide(lax.ppermute(narrow(held), frame_axes, fold))
    before = jnp.zeros_like(held)
    for k in (1, 2, 4):
        sent = narrow(column)
        if k == 2:
            sent, prev_first = lax.optimization_barrier((sent, prev_first))
        if k == 1:
            up_edge, down_edge = edges(hidden, frames - 1, (), time_weight, sent)
            top, bottom = ahead(down_edge, "row", 1), ahead(up_edge, "row", -1)
            ffn_out = conv_frame(hidden, frames - 1, (), top, bottom, weights)
        pairs = [
            (z * INNER + at, (z + k) * INNER + at)
            for z in range(planes - k)
            for at in range(INNER - 1)
        ]
        arrived = lax.ppermute(sent, frame_axes, pairs)
        if k == 4:
            arrived, ffn_out = lax.optimization_barrier((arrived, ffn_out))
        column = column + wide(arrived)
        before = before + wide(arrived)
    prefix = before + held
    closed, opened = lax.optimization_barrier((narrow(prefix), narrow(before), prev_last))[:2]
    up_edge, down_edge = edges(hidden, 0, (prev_first, prev_last), time_weight, closed)
    top_first, bottom_first = ahead(down_edge, "row", 1), ahead(up_edge, "row", -1)
    for k in range(1, INNER):
        sent = jnp.where(x + k < INNER, closed, opened)
        prefix = prefix + wide(ahead(sent, "x", k, True))
    prefix = narrow(prefix)
    prev_middle, _ = copied_rows(hidden, frames - 1, (1,), prefix)
    prev_middle = ahead(prev_middle, frame_axes, 1)

    state = jnp.concatenate([prefix, exchange(prefix, "row", 4)], axis=0)
    state = jnp.concatenate([state, exchange(state, "row", 2)], axis=0)
    state, prev_middle = lax.optimization_barrier((state, prev_middle))
    state = jnp.concatenate([state, exchange(state, "row", 1)], axis=0)
    attention = whole(
        mixed_kernel,
        jax.ShapeDtypeStruct((tokens, width), jnp.bfloat16),
        2 * tokens * width * 256,
        row,
        query_tokens.reshape(tokens, width),
        state,
        norm_gain[None],
    )
    ffn_out = conv_frame(
        hidden, 0, (prev_first, prev_middle, prev_last), top_first, bottom_first, weights, ffn_out
    )
    return (attention.reshape(query_tokens.shape), ffn_out)


def solution(mesh):
    frame, row = mesh.shape["frame"], mesh.shape["row"]
    split = Mesh(mesh.devices.reshape(frame // INNER, INNER, row), ("z", "x", "row"))
    tokens = P(("z", "x"), "row", None, None)
    return jax.shard_map(
        per_device,
        mesh=split,
        in_specs=(tokens, tokens, tokens, P(), tokens, P(), P(), P()),
        out_specs=(tokens, tokens),
        check_vma=False,
    )
```

```python
import functools

import jax
import jax.numpy as jnp
from jax import lax
from jax.experimental import pallas as pl
from jax.experimental.pallas import tpu as pltpu
from jax.sharding import Mesh, PartitionSpec as P

HD = 112
FF = 5600
LANES = 128
UNIT = 16
SHARES = 8
SHARE_ROWS = 256
INNER = 4
PARTS = 4
epsilon = 1e-06


def windows(width):
    out = []
    for head in range(width // HD):
        tile, offset = divmod(head * HD, LANES)
        span = LANES if offset + HD <= LANES else 2 * LANES
        out.append((tile, offset, min(span, width - tile * LANES)))
    return out


def unit_row(unit, row):
    share, inside = divmod(unit, UNIT)
    place = share ^ row
    place = ((place & 1) << 2) | (place & 2) | (place >> 2)
    return pl.multiple_of(place * SHARE_ROWS + inside * UNIT, UNIT)


def partial_kernel(row_ref, key_ref, value_ref, token_ref, out_ref):
    row = row_ref[0]
    width = key_ref.shape[1]
    pending = {}

    def flush(tile):
        rounded = pending.pop(tile).astype(jnp.bfloat16)
        for piece in range(HD // UNIT):
            out_ref[pl.ds(unit_row(tile * (HD // UNIT) + piece, row), UNIT), :] = rounded[
                piece * UNIT : (piece + 1) * UNIT
            ]

    for tile, offset, span in windows(width):
        lanes = slice(tile * LANES, tile * LANES + span)
        keys = jnp.maximum(key_ref[:, lanes], 0)
        product = lax.dot_general(
            keys, value_ref[:, lanes], (((0,), (0,)), ((), ())), preferred_element_type=jnp.float32
        )
        block = product[offset : offset + HD]
        lane = lax.broadcasted_iota(jnp.int32, block.shape, 1)
        block = jnp.where((lane >= offset) & (lane < offset + HD), block, 0.0)
        for old in [done for done in pending if done < tile]:
            flush(old)
        for step in range(pl.cdiv(span, LANES)):
            part = block[:, step * LANES : min(span, (step + 1) * LANES)]
            if part.shape[1] < LANES:
                part = jnp.concatenate(
                    [part, jnp.zeros((HD, LANES - part.shape[1]), jnp.float32)], axis=1
                )
            at = tile + step
            pending[at] = pending[at] + part if at in pending else part
    tiles = max(pending) + 1
    for old in sorted(pending):
        flush(old)
    for unit in range(tiles * (HD // UNIT), SHARES * UNIT):
        out_ref[pl.ds(unit_row(unit, row), UNIT), :] = jnp.zeros((UNIT, LANES), jnp.bfloat16)


def mixed_kernel(row_ref, query_ref, state_ref, gain_ref, out_ref):
    row = row_ref[0]
    tokens, width = query_ref.shape
    pending = {}

    def state_tile(tile):
        return jnp.concatenate(
            [
                state_ref[pl.ds(unit_row(tile * (HD // UNIT) + piece, row), UNIT), :]
                for piece in range(HD // UNIT)
            ],
            axis=0,
        )

    def flush(tile):
        lanes = slice(tile * LANES, min(width, (tile + 1) * LANES))
        count = lanes.stop - lanes.start
        out_ref[:, lanes] = (pending.pop(tile)[:, :count] * gain_ref[:, lanes]).astype(jnp.bfloat16)

    for tile, offset, span in windows(width):
        lanes = slice(tile * LANES, tile * LANES + span)
        steps = pl.cdiv(span, LANES)
        block = jnp.concatenate([state_tile(tile + step) for step in range(steps)], axis=1)
        lane = lax.broadcasted_iota(jnp.int32, block.shape, 1)
        block = jnp.where((lane >= offset) & (lane < offset + HD), block, jnp.zeros_like(block))
        pieces = [block]
        if offset:
            pieces.insert(0, jnp.zeros((offset, block.shape[1]), jnp.bfloat16))
        if span - offset - HD:
            pieces.append(jnp.zeros((span - offset - HD, block.shape[1]), jnp.bfloat16))
        right = jnp.concatenate(pieces, axis=0) if len(pieces) > 1 else block
        mixed = jnp.dot(
            jnp.maximum(query_ref[:, lanes], 0), right, preferred_element_type=jnp.float32
        )
        mean_square = jnp.sum(mixed * mixed, axis=1, keepdims=True) * (1.0 / HD)
        normed = mixed * lax.rsqrt(mean_square + epsilon)
        for old in [done for done in pending if done < tile]:
            flush(old)
        for step in range(steps):
            part = normed[:, step * LANES : (step + 1) * LANES]
            at = tile + step
            pending[at] = pending[at] + part if at in pending else part
    for old in sorted(pending):
        flush(old)


def conv_kernel(frame, own_ref, *refs):
    *_, out_ref, held_ref, done_ref, sems, held_sems = refs
    if frame:
        prev_refs = [held_ref.at[0, r] for r in range(own_ref.shape[1])]
    else:
        ends_ref, middle_ref, *refs = refs
        prev_refs = [ends_ref.at[0], middle_ref.at[0], ends_ref.at[1]]
    top_ref, bottom_ref, time_ref, space_ref, bias_ref = refs[:5]
    cur_ref = held_ref.at[-1 % held_ref.shape[0]]
    rows, columns, channels = cur_ref.shape
    groups = columns // 8
    skew = FF % LANES
    lead = FF // LANES
    bounds = [0, lead // 14, lead // 4, lead * 5 // 8, lead]
    fetches = []
    for part, (start, stop) in enumerate(zip(bounds, bounds[1:])):
        gate_start = lead + start + (part > 0)
        gate_stop = min(channels, (lead + stop + 1) * LANES) if part < PARTS - 1 else channels
        spans = (start * LANES, stop * LANES), (gate_start * LANES, gate_stop)
        fetches.append(
            [
                pltpu.make_async_copy(
                    own_ref.at[pl.ds(0, held_ref.shape[0]), :, :, pl.ds(a, b - a)],
                    held_ref.at[:, :, :, pl.ds(a, b - a)],
                    held_sems.at[part, which],
                )
                for which, (a, b) in enumerate(spans)
            ]
        )
        for fetch in fetches[-1]:
            fetch.start()

    def conv_tile(lanes):
        times = time_ref[:, lanes]
        lines = [times[0:1], times[1:2]]
        for a in range(3):
            taps = space_ref[a, :, lanes]
            lines += [taps[b : b + 1] for b in range(3)]
        lines.append(bias_ref[:, lanes])
        shape = (8, lines[0].shape[1])
        pick = [jnp.broadcast_to(line, shape) for line in lines]
        subrow = lax.broadcasted_iota(jnp.int32, shape, 0)
        first, last = subrow == 0, subrow == 7
        zero = jnp.zeros(shape, jnp.float32)

        def split(value):
            return [value[8 * g : 8 * g + 8] for g in range(groups)]

        spread = [split(top_ref[0, :, lanes].astype(jnp.float32))]
        for r in range(rows):
            now = split(cur_ref[r, :, lanes].astype(jnp.float32))
            old = split(prev_refs[r][:, lanes].astype(jnp.float32))
            blend = jnp.concatenate([pick[0] * c + pick[1] * p for c, p in zip(now, old)], axis=0)
            spread.append(split(blend.astype(jnp.bfloat16).astype(jnp.float32)))
        spread.append(split(bottom_ref[0, :, lanes].astype(jnp.float32)))
        out = []
        for r in range(rows):
            sums = []
            for b in range(3):
                sums.append(
                    [
                        pick[2 + b] * spread[r][g]
                        + pick[5 + b] * spread[r + 1][g]
                        + pick[8 + b] * spread[r + 2][g]
                        for g in range(groups)
                    ]
                )
            left = [zero] + [pltpu.roll(value, 1, 0) for value in sums[0]]
            right = [pltpu.roll(value, 7, 0) for value in sums[2]] + [zero]
            out += [
                (pick[11] + sums[1][g])
                + jnp.where(first, left[g], left[g + 1])
                + jnp.where(last, right[g + 1], right[g])
                for g in range(groups)
            ]
        return out

    lane = lax.broadcasted_iota(jnp.int32, (8, LANES), 1)

    def gates(lanes):
        turned = []
        for value in conv_tile(lanes):
            value = value * (1.0 / (1.0 + jnp.exp(-value)))
            if value.shape[1] < LANES:
                rest = jnp.zeros((8, LANES - value.shape[1]), jnp.float32)
                value = jnp.concatenate([value, rest], axis=1)
            turned.append(pltpu.roll(value, LANES - skew, 1))
        return turned

    def step(lanes, near, far, width):
        values = conv_tile(lanes)
        gated = [
            value * jnp.where(lane < LANES - skew, a, b) for value, a, b in zip(values, near, far)
        ]
        for r in range(rows):
            row = jnp.concatenate(gated[r * groups : (r + 1) * groups], axis=0)
            row = row.astype(jnp.bfloat16)
            done_ref[r, :, pl.ds(lanes.start, width)] = row[:, :width]

    def tile_at(index):
        return pl.ds(pl.multiple_of(index * LANES, LANES), LANES)

    def body(tile, near):
        far = gates(tile_at(tile + lead + 1))
        step(tile_at(tile), near, far, LANES)
        return far

    near = None
    for part, (start, stop) in enumerate(zip(bounds, bounds[1:])):
        for fetch in fetches[part]:
            fetch.wait()
        if near is None:
            near = gates(pl.ds(lead * LANES, LANES))
        near = lax.fori_loop(start, stop, body, near)
    last = (lead * 2 + 1) * LANES
    far = gates(pl.ds(last, channels - last))
    step(pl.ds(lead * LANES, LANES), near, far, skew)
    copies = [
        pltpu.make_async_copy(done_ref.at[r], out_ref.at[frame, r], sems.at[r]) for r in range(rows)
    ]
    for copy in copies:
        copy.start()
    for copy in copies:
        copy.wait()


def conv_frame(hidden, frame, prev, top, bottom, weights, into=None):
    frames, rows, columns, channels = hidden.shape
    args = [hidden, *prev, top, bottom, *weights]
    specs = [pl.BlockSpec(memory_space=pltpu.VMEM)] * len(args)
    args[0] = pltpu.with_memory_space_constraint(hidden, pltpu.HBM)
    specs[0] = pl.BlockSpec(memory_space=pl.ANY)
    aliases = {}
    if into is not None:
        aliases = {len(args): 0}
        args.append(into)
        specs.append(pl.BlockSpec(memory_space=pl.ANY))
    elements = rows * columns * channels
    return pl.pallas_call(
        functools.partial(conv_kernel, frame),
        out_shape=jax.ShapeDtypeStruct((frames, rows, columns, FF), jnp.bfloat16),
        in_specs=specs,
        out_specs=pl.BlockSpec(memory_space=pl.ANY),
        scratch_shapes=[
            pltpu.VMEM((frame + 1, rows, columns, channels), jnp.bfloat16),
            pltpu.VMEM((rows, columns, FF), jnp.bfloat16),
            pltpu.SemaphoreType.DMA((rows,)),
            pltpu.SemaphoreType.DMA((PARTS, 2)),
        ],
        input_output_aliases=aliases,
        compiler_params=pltpu.CompilerParams(vmem_limit_bytes=12 << 20),
        cost_estimate=pl.CostEstimate(
            flops=elements * 40, bytes_accessed=elements * 6, transcendentals=elements // 2
        ),
        name="conv_frame",
    )(*args)


def row_copies(source_ref, target_ref, sems):
    return [
        pltpu.make_async_copy(
            source_ref.at[pl.ds(8 * g, 8)], target_ref.at[pl.ds(8 * g, 8)], sems.at[g]
        )
        for g in range(source_ref.shape[0] // 8)
    ]


def edge_kernel(own_ref, *refs, frame):
    up_ref, down_ref, token_ref, now_ref, old_ref, sems = refs[-6:]
    ends_ref, time_ref = (None, refs[0]) if frame else refs[:2]
    token_ref[...] = jnp.zeros_like(token_ref)
    rows, channels = own_ref.shape[1], own_ref.shape[3]
    ends = (0, rows - 1)
    copies = []
    for at, r in enumerate(ends):
        group = row_copies(own_ref.at[frame, r], now_ref.at[at], sems.at[0, at])
        if frame:
            group += row_copies(own_ref.at[frame - 1, r], old_ref.at[at], sems.at[1, at])
        copies.append(group)
    for copy in copies[0] + copies[1]:
        copy.start()

    for at, out_ref in enumerate((up_ref, down_ref)):
        old_view = old_ref.at[at] if frame else ends_ref.at[at]
        for copy in copies[at]:
            copy.wait()

        def blend(lanes):
            times = time_ref[:, lanes]
            now = now_ref[at, :, lanes].astype(jnp.float32)
            old = old_view[:, lanes].astype(jnp.float32)
            out_ref[0, :, lanes] = (times[0:1] * now + times[1:2] * old).astype(jnp.bfloat16)

        wide = 4 * LANES

        @pl.loop(0, channels // wide)
        def _(tile):
            blend(pl.ds(pl.multiple_of(tile * wide, LANES), wide))

        if channels % wide:
            blend(pl.ds(channels // wide * wide, channels % wide))


def edges(hidden, frame, old, times, *waits):
    channels, columns = hidden.shape[3], hidden.shape[2]
    held = pl.BlockSpec(memory_space=pltpu.VMEM)
    anywhere = pl.BlockSpec(memory_space=pl.ANY)
    args = [pltpu.with_memory_space_constraint(hidden, pltpu.HBM), *old, times, *waits]
    line = jax.ShapeDtypeStruct((1, columns, channels), jnp.bfloat16)
    pair = pltpu.VMEM((2, columns, channels), jnp.bfloat16)
    return pl.pallas_call(
        functools.partial(edge_kernel, frame=frame),
        out_shape=(line, line, jax.ShapeDtypeStruct((8, LANES), jnp.float32)),
        in_specs=[anywhere] + [held] * (len(old) + 1) + [anywhere] * len(waits),
        out_specs=(held, held, held),
        scratch_shapes=[pair, pair, pltpu.SemaphoreType.DMA((2, 2, columns // 8))],
        compiler_params=pltpu.CompilerParams(vmem_limit_bytes=8 << 20),
        cost_estimate=pl.CostEstimate(
            flops=6 * columns * channels, bytes_accessed=12 * columns * channels, transcendentals=0
        ),
        name="edges",
    )(*args)


def copy_kernel(source_ref, *refs, frame, rows):
    *_, token_ref, sems = refs
    out_ref = refs[-3]
    copies = []
    for at, r in enumerate(rows):
        copies += row_copies(source_ref.at[frame, r], out_ref.at[at], sems.at[at])
    for copy in copies:
        copy.start()
    token_ref[...] = jnp.zeros_like(token_ref)
    for copy in copies:
        copy.wait()


def copied_rows(hidden, frame, rows, *tokens):
    _, _, columns, channels = hidden.shape
    args = (pltpu.with_memory_space_constraint(hidden, pltpu.HBM), *tokens)
    anywhere = pl.BlockSpec(memory_space=pl.ANY)
    return pl.pallas_call(
        functools.partial(copy_kernel, frame=frame, rows=rows),
        out_shape=(
            jax.ShapeDtypeStruct((len(rows), columns, channels), jnp.bfloat16),
            jax.ShapeDtypeStruct((8, LANES), jnp.float32),
        ),
        in_specs=[anywhere] * len(args),
        out_specs=(pl.BlockSpec(memory_space=pltpu.VMEM),) * 2,
        scratch_shapes=[pltpu.SemaphoreType.DMA((len(rows), columns // 8))],
        cost_estimate=pl.CostEstimate(
            flops=0, bytes_accessed=4 * len(rows) * columns * channels, transcendentals=0
        ),
        name="copied_rows",
    )(*args)


def reached_kernel(*refs):
    refs[-1][...] = jnp.zeros_like(refs[-1])


def reached(*arrays):
    return pl.pallas_call(
        reached_kernel,
        out_shape=jax.ShapeDtypeStruct((8, LANES), jnp.float32),
        in_specs=[pl.BlockSpec(memory_space=pltpu.VMEM)] * len(arrays),
        out_specs=pl.BlockSpec(memory_space=pltpu.VMEM),
        name="reached",
    )(*arrays)


def whole(body, out_shape, flops, *args, token=None):
    specs = [pl.BlockSpec(memory_space=pltpu.SMEM)]
    specs += [pl.BlockSpec(memory_space=pltpu.VMEM)] * (len(args) - 1)
    if token is not None:
        args += (token,)
        specs.append(pl.BlockSpec(memory_space=pl.ANY))
    return pl.pallas_call(
        body,
        out_shape=out_shape,
        in_specs=specs,
        out_specs=pl.BlockSpec(memory_space=pltpu.VMEM),
        compiler_params=pltpu.CompilerParams(vmem_limit_bytes=10 << 20),
        cost_estimate=pl.CostEstimate(flops=flops, bytes_accessed=3 << 20, transcendentals=0),
        name=body.__name__,
    )(*args)


def exchange(value, axis, flip):
    return lax.ppermute(value, axis, [(i, i ^ flip) for i in range(lax.axis_size(axis))])


def ahead(value, axis, steps, wrap=False):
    count = lax.axis_size(axis)
    pairs = [(i, (i + steps) % count) for i in range(count) if wrap or 0 <= i + steps < count]
    return lax.ppermute(value, axis, pairs)


def per_device(
    query_tokens, key_tokens, value_tokens, norm_gain, hidden, time_weight, space_weight, conv_bias
):
    frames, rows, columns, width = query_tokens.shape
    tokens = frames * rows * columns
    channels = hidden.shape[3]
    frame_axes = ("z", "x")
    row = lax.axis_index("row").astype(jnp.int32).reshape(1)
    x = lax.axis_index("x")
    narrow = lambda value: value.astype(jnp.bfloat16)
    wide = lambda value: value.astype(jnp.float32)

    weights = time_weight, space_weight, conv_bias[None]
    prev_ends, token = copied_rows(hidden, frames - 1, (0, rows - 1))
    prev_ends = ahead(prev_ends, frame_axes, 1)
    partial = whole(
        partial_kernel,
        jax.ShapeDtypeStruct((SHARES * SHARE_ROWS, LANES), jnp.bfloat16),
        2 * tokens * width * 256,
        row,
        key_tokens.reshape(tokens, width),
        value_tokens.reshape(tokens, width),
        token=token,
    )
    held = partial.reshape(2, 4, SHARE_ROWS, LANES)
    held = wide(held[0]) + wide(exchange(held[1], "row", 1))
    held = held[:2] + wide(exchange(narrow(held[2:]), "row", 2))
    held = held[0] + wide(exchange(narrow(held[1]), "row", 4))

    planes = lax.axis_size("z")
    fold = [(z * INNER + INNER - 1, z * INNER + INNER - 2) for z in range(planes)]
    column = held + wide(lax.ppermute(narrow(held), frame_axes, fold))
    before = jnp.zeros_like(held)
    for k in (1, 2, 4):
        sent = narrow(column)
        if k == 2:
            up_edge, down_edge, edge_token = edges(hidden, frames - 1, (), time_weight, sent)
            top, bottom = ahead(down_edge, "row", 1), ahead(up_edge, "row", -1)
            ffn_out = conv_frame(hidden, frames - 1, (), top, bottom, weights)
            sent, edge_token = lax.optimization_barrier((sent, edge_token))
        if k == 4:
            prev_middle, copy_token = copied_rows(hidden, frames - 1, (1,), sent, edge_token)
        pairs = [
            (z * INNER + at, (z + k) * INNER + at)
            for z in range(planes - k)
            for at in range(INNER - 1)
        ]
        arrived = lax.ppermute(sent, frame_axes, pairs)
        column = column + wide(arrived)
        before = before + wide(arrived)
    prefix = before + held
    edge_token = reached(top, bottom, copy_token)
    closed, opened, prev_ends, edge_token = lax.optimization_barrier(
        (narrow(prefix), narrow(before), prev_ends, edge_token)
    )
    for k in range(1, INNER):
        sent = jnp.where(x + k < INNER, closed, opened)
        prefix = prefix + wide(ahead(sent, "x", k, True))
    prefix = narrow(prefix)
    prev_middle = ahead(lax.optimization_barrier((prev_middle, prefix))[0], frame_axes, 1)
    up_edge, down_edge, _ = edges(hidden, 0, (prev_ends,), time_weight, prefix, edge_token)
    top_first, bottom_first = ahead(down_edge, "row", 1), ahead(up_edge, "row", -1)

    state = jnp.concatenate([prefix, exchange(prefix, "row", 4)], axis=0)
    state = jnp.concatenate([state, exchange(state, "row", 2)], axis=0)
    state, prev_middle, ffn_out = lax.optimization_barrier((state, prev_middle, ffn_out))
    state = jnp.concatenate([state, exchange(state, "row", 1)], axis=0)
    attention = whole(
        mixed_kernel,
        jax.ShapeDtypeStruct((tokens, width), jnp.bfloat16),
        2 * tokens * width * 256,
        row,
        query_tokens.reshape(tokens, width),
        state,
        norm_gain[None],
    )
    ffn_out = conv_frame(
        hidden, 0, (prev_ends, prev_middle), top_first, bottom_first, weights, ffn_out
    )
    return (attention.reshape(query_tokens.shape), ffn_out)


def solution(mesh):
    frame, row = mesh.shape["frame"], mesh.shape["row"]
    split = Mesh(mesh.devices.reshape(frame // INNER, INNER, row), ("z", "x", "row"))
    tokens = P(("z", "x"), "row", None, None)
    return jax.shard_map(
        per_device,
        mesh=split,
        in_specs=(tokens, tokens, tokens, P(), tokens, P(), P(), P()),
        out_specs=(tokens, tokens),
        check_vma=False,
    )
```

```python
import functools

import jax
import jax.numpy as jnp
from jax import lax
from jax.experimental import pallas as pl
from jax.experimental.pallas import tpu as pltpu
from jax.sharding import Mesh, PartitionSpec as P

HD = 112
FF = 5600
LANES = 128
UNIT = 16
SHARES = 8
SHARE_ROWS = 256
INNER = 4
PARTS = 4
epsilon = 1e-06


def windows(width):
    out = []
    for head in range(width // HD):
        tile, offset = divmod(head * HD, LANES)
        span = LANES if offset + HD <= LANES else 2 * LANES
        out.append((tile, offset, min(span, width - tile * LANES)))
    return out


def unit_row(unit, row):
    share, inside = divmod(unit, UNIT)
    place = share ^ row
    place = ((place & 1) << 2) | (place & 2) | (place >> 2)
    return pl.multiple_of(place * SHARE_ROWS + inside * UNIT, UNIT)


def partial_kernel(row_ref, key_ref, value_ref, token_ref, out_ref):
    row = row_ref[0]
    width = key_ref.shape[1]
    pending = {}

    def flush(tile):
        rounded = pending.pop(tile).astype(jnp.bfloat16)
        for piece in range(HD // UNIT):
            out_ref[pl.ds(unit_row(tile * (HD // UNIT) + piece, row), UNIT), :] = rounded[
                piece * UNIT : (piece + 1) * UNIT
            ]

    for tile, offset, span in windows(width):
        lanes = slice(tile * LANES, tile * LANES + span)
        keys = jnp.maximum(key_ref[:, lanes], 0)
        product = lax.dot_general(
            keys, value_ref[:, lanes], (((0,), (0,)), ((), ())), preferred_element_type=jnp.float32
        )
        block = product[offset : offset + HD]
        lane = lax.broadcasted_iota(jnp.int32, block.shape, 1)
        block = jnp.where((lane >= offset) & (lane < offset + HD), block, 0.0)
        for old in [done for done in pending if done < tile]:
            flush(old)
        for step in range(pl.cdiv(span, LANES)):
            part = block[:, step * LANES : min(span, (step + 1) * LANES)]
            if part.shape[1] < LANES:
                part = jnp.concatenate(
                    [part, jnp.zeros((HD, LANES - part.shape[1]), jnp.float32)], axis=1
                )
            at = tile + step
            pending[at] = pending[at] + part if at in pending else part
    tiles = max(pending) + 1
    for old in sorted(pending):
        flush(old)
    for unit in range(tiles * (HD // UNIT), SHARES * UNIT):
        out_ref[pl.ds(unit_row(unit, row), UNIT), :] = jnp.zeros((UNIT, LANES), jnp.bfloat16)


def mixed_kernel(row_ref, query_ref, state_ref, gain_ref, out_ref):
    row = row_ref[0]
    tokens, width = query_ref.shape
    pending = {}

    def state_tile(tile):
        return jnp.concatenate(
            [
                state_ref[pl.ds(unit_row(tile * (HD // UNIT) + piece, row), UNIT), :]
                for piece in range(HD // UNIT)
            ],
            axis=0,
        )

    def flush(tile):
        lanes = slice(tile * LANES, min(width, (tile + 1) * LANES))
        count = lanes.stop - lanes.start
        out_ref[:, lanes] = (pending.pop(tile)[:, :count] * gain_ref[:, lanes]).astype(jnp.bfloat16)

    for tile, offset, span in windows(width):
        lanes = slice(tile * LANES, tile * LANES + span)
        steps = pl.cdiv(span, LANES)
        block = jnp.concatenate([state_tile(tile + step) for step in range(steps)], axis=1)
        lane = lax.broadcasted_iota(jnp.int32, block.shape, 1)
        block = jnp.where((lane >= offset) & (lane < offset + HD), block, jnp.zeros_like(block))
        pieces = [block]
        if offset:
            pieces.insert(0, jnp.zeros((offset, block.shape[1]), jnp.bfloat16))
        if span - offset - HD:
            pieces.append(jnp.zeros((span - offset - HD, block.shape[1]), jnp.bfloat16))
        right = jnp.concatenate(pieces, axis=0) if len(pieces) > 1 else block
        mixed = jnp.dot(
            jnp.maximum(query_ref[:, lanes], 0), right, preferred_element_type=jnp.float32
        )
        mean_square = jnp.sum(mixed * mixed, axis=1, keepdims=True) * (1.0 / HD)
        normed = mixed * lax.rsqrt(mean_square + epsilon)
        for old in [done for done in pending if done < tile]:
            flush(old)
        for step in range(steps):
            part = normed[:, step * LANES : (step + 1) * LANES]
            at = tile + step
            pending[at] = pending[at] + part if at in pending else part
    for old in sorted(pending):
        flush(old)


def conv_kernel(frame, own_ref, *refs):
    *_, out_ref, held_ref, done_ref, sems, held_sems = refs
    if frame:
        prev_refs = [held_ref.at[0, r] for r in range(own_ref.shape[1])]
    else:
        prev_refs, refs = [ref.at[0] for ref in refs[:3]], refs[3:]
    top_ref, bottom_ref, time_ref, space_ref, bias_ref = refs[:5]
    cur_ref = held_ref.at[-1 % held_ref.shape[0]]
    rows, columns, channels = cur_ref.shape
    groups = columns // 8
    skew = FF % LANES
    lead = FF // LANES
    bounds = [0, lead // 14, lead // 4, lead * 5 // 8, lead]
    fetches = []
    for part, (start, stop) in enumerate(zip(bounds, bounds[1:])):
        gate_start = lead + start + (part > 0)
        gate_stop = min(channels, (lead + stop + 1) * LANES) if part < PARTS - 1 else channels
        spans = (start * LANES, stop * LANES), (gate_start * LANES, gate_stop)
        fetches.append(
            [
                pltpu.make_async_copy(
                    own_ref.at[pl.ds(0, held_ref.shape[0]), :, :, pl.ds(a, b - a)],
                    held_ref.at[:, :, :, pl.ds(a, b - a)],
                    held_sems.at[part, which],
                )
                for which, (a, b) in enumerate(spans)
            ]
        )
        for fetch in fetches[-1]:
            fetch.start()

    def conv_tile(lanes):
        times = time_ref[:, lanes]
        lines = [times[0:1], times[1:2]]
        for a in range(3):
            taps = space_ref[a, :, lanes]
            lines += [taps[b : b + 1] for b in range(3)]
        lines.append(bias_ref[:, lanes])
        shape = (8, lines[0].shape[1])
        pick = [jnp.broadcast_to(line, shape) for line in lines]
        subrow = lax.broadcasted_iota(jnp.int32, shape, 0)
        first, last = subrow == 0, subrow == 7
        zero = jnp.zeros(shape, jnp.float32)

        def split(value):
            return [value[8 * g : 8 * g + 8] for g in range(groups)]

        spread = [split(top_ref[0, :, lanes].astype(jnp.float32))]
        for r in range(rows):
            now = split(cur_ref[r, :, lanes].astype(jnp.float32))
            old = split(prev_refs[r][:, lanes].astype(jnp.float32))
            blend = jnp.concatenate([pick[0] * c + pick[1] * p for c, p in zip(now, old)], axis=0)
            spread.append(split(blend.astype(jnp.bfloat16).astype(jnp.float32)))
        spread.append(split(bottom_ref[0, :, lanes].astype(jnp.float32)))
        out = []
        for r in range(rows):
            sums = []
            for b in range(3):
                sums.append(
                    [
                        pick[2 + b] * spread[r][g]
                        + pick[5 + b] * spread[r + 1][g]
                        + pick[8 + b] * spread[r + 2][g]
                        for g in range(groups)
                    ]
                )
            left = [zero] + [pltpu.roll(value, 1, 0) for value in sums[0]]
            right = [pltpu.roll(value, 7, 0) for value in sums[2]] + [zero]
            out += [
                (pick[11] + sums[1][g])
                + jnp.where(first, left[g], left[g + 1])
                + jnp.where(last, right[g + 1], right[g])
                for g in range(groups)
            ]
        return out

    lane = lax.broadcasted_iota(jnp.int32, (8, LANES), 1)

    def gates(lanes):
        turned = []
        for value in conv_tile(lanes):
            value = value * (1.0 / (1.0 + jnp.exp(-value)))
            if value.shape[1] < LANES:
                rest = jnp.zeros((8, LANES - value.shape[1]), jnp.float32)
                value = jnp.concatenate([value, rest], axis=1)
            turned.append(pltpu.roll(value, LANES - skew, 1))
        return turned

    def step(lanes, near, far, width):
        values = conv_tile(lanes)
        gated = [
            value * jnp.where(lane < LANES - skew, a, b) for value, a, b in zip(values, near, far)
        ]
        for r in range(rows):
            row = jnp.concatenate(gated[r * groups : (r + 1) * groups], axis=0)
            row = row.astype(jnp.bfloat16)
            done_ref[r, :, pl.ds(lanes.start, width)] = row[:, :width]

    def tile_at(index):
        return pl.ds(pl.multiple_of(index * LANES, LANES), LANES)

    def body(tile, near):
        far = gates(tile_at(tile + lead + 1))
        step(tile_at(tile), near, far, LANES)
        return far

    near = None
    for part, (start, stop) in enumerate(zip(bounds, bounds[1:])):
        for fetch in fetches[part]:
            fetch.wait()
        if near is None:
            near = gates(pl.ds(lead * LANES, LANES))
        near = lax.fori_loop(start, stop, body, near)
    last = (lead * 2 + 1) * LANES
    far = gates(pl.ds(last, channels - last))
    step(pl.ds(lead * LANES, LANES), near, far, skew)
    copies = [
        pltpu.make_async_copy(done_ref.at[r], out_ref.at[frame, r], sems.at[r]) for r in range(rows)
    ]
    for copy in copies:
        copy.start()
    for copy in copies:
        copy.wait()


def conv_frame(hidden, frame, prev, top, bottom, weights, into=None):
    frames, rows, columns, channels = hidden.shape
    args = [hidden, *prev, top, bottom, *weights]
    specs = [pl.BlockSpec(memory_space=pltpu.VMEM)] * len(args)
    args[0] = pltpu.with_memory_space_constraint(hidden, pltpu.HBM)
    specs[0] = pl.BlockSpec(memory_space=pl.ANY)
    aliases = {}
    if into is not None:
        aliases = {len(args): 0}
        args.append(into)
        specs.append(pl.BlockSpec(memory_space=pl.ANY))
    elements = rows * columns * channels
    return pl.pallas_call(
        functools.partial(conv_kernel, frame),
        out_shape=jax.ShapeDtypeStruct((frames, rows, columns, FF), jnp.bfloat16),
        in_specs=specs,
        out_specs=pl.BlockSpec(memory_space=pl.ANY),
        scratch_shapes=[
            pltpu.VMEM((frame + 1, rows, columns, channels), jnp.bfloat16),
            pltpu.VMEM((rows, columns, FF), jnp.bfloat16),
            pltpu.SemaphoreType.DMA((rows,)),
            pltpu.SemaphoreType.DMA((PARTS, 2)),
        ],
        input_output_aliases=aliases,
        compiler_params=pltpu.CompilerParams(vmem_limit_bytes=12 << 20),
        cost_estimate=pl.CostEstimate(
            flops=elements * 40, bytes_accessed=elements * 6, transcendentals=elements // 2
        ),
        name="conv_frame",
    )(*args)


def row_copies(source_ref, target_ref, sems):
    return [
        pltpu.make_async_copy(
            source_ref.at[pl.ds(8 * g, 8)], target_ref.at[pl.ds(8 * g, 8)], sems.at[g]
        )
        for g in range(source_ref.shape[0] // 8)
    ]


def edge_kernel(own_ref, *refs, frame):
    up_ref, down_ref, token_ref, now_ref, old_ref, sems = refs[-6:]
    old_refs, time_ref = (refs[:0], refs[0]) if frame else (refs[:2], refs[2])
    token_ref[...] = jnp.zeros_like(token_ref)
    rows, channels = own_ref.shape[1], own_ref.shape[3]
    ends = (0, rows - 1)
    copies = []
    for at, r in enumerate(ends):
        group = row_copies(own_ref.at[frame, r], now_ref.at[at], sems.at[0, at])
        if frame:
            group += row_copies(own_ref.at[frame - 1, r], old_ref.at[at], sems.at[1, at])
        copies.append(group)
    for copy in copies[0] + copies[1]:
        copy.start()

    for at, out_ref in enumerate((up_ref, down_ref)):
        old_view = old_ref.at[at] if frame else old_refs[at].at[0]
        for copy in copies[at]:
            copy.wait()

        def blend(lanes):
            times = time_ref[:, lanes]
            now = now_ref[at, :, lanes].astype(jnp.float32)
            old = old_view[:, lanes].astype(jnp.float32)
            out_ref[0, :, lanes] = (times[0:1] * now + times[1:2] * old).astype(jnp.bfloat16)

        wide = 4 * LANES

        @pl.loop(0, channels // wide)
        def _(tile):
            blend(pl.ds(pl.multiple_of(tile * wide, LANES), wide))

        if channels % wide:
            blend(pl.ds(channels // wide * wide, channels % wide))


def edges(hidden, frame, old, times, *waits):
    channels, columns = hidden.shape[3], hidden.shape[2]
    held = pl.BlockSpec(memory_space=pltpu.VMEM)
    anywhere = pl.BlockSpec(memory_space=pl.ANY)
    args = [pltpu.with_memory_space_constraint(hidden, pltpu.HBM), *old, times, *waits]
    line = jax.ShapeDtypeStruct((1, columns, channels), jnp.bfloat16)
    pair = pltpu.VMEM((2, columns, channels), jnp.bfloat16)
    return pl.pallas_call(
        functools.partial(edge_kernel, frame=frame),
        out_shape=(line, line, jax.ShapeDtypeStruct((8, LANES), jnp.float32)),
        in_specs=[anywhere] + [held] * (len(old) + 1) + [anywhere] * len(waits),
        out_specs=(held, held, held),
        scratch_shapes=[pair, pair, pltpu.SemaphoreType.DMA((2, 2, columns // 8))],
        compiler_params=pltpu.CompilerParams(vmem_limit_bytes=8 << 20),
        cost_estimate=pl.CostEstimate(
            flops=6 * columns * channels, bytes_accessed=12 * columns * channels, transcendentals=0
        ),
        name="edges",
    )(*args)


def copy_kernel(source_ref, *refs, frame, rows):
    *_, token_ref, sems = refs
    outs = refs[-2 - len(rows) : -2]
    copies = []
    for at, (r, out_ref) in enumerate(zip(rows, outs)):
        copies += row_copies(source_ref.at[frame, r], out_ref.at[0], sems.at[at])
    for copy in copies:
        copy.start()
    token_ref[...] = jnp.zeros_like(token_ref)
    for copy in copies:
        copy.wait()


def copied_rows(hidden, frame, rows, *tokens):
    _, _, columns, channels = hidden.shape
    args = (pltpu.with_memory_space_constraint(hidden, pltpu.HBM), *tokens)
    anywhere = pl.BlockSpec(memory_space=pl.ANY)
    return pl.pallas_call(
        functools.partial(copy_kernel, frame=frame, rows=rows),
        out_shape=[jax.ShapeDtypeStruct((1, columns, channels), jnp.bfloat16) for _ in rows]
        + [jax.ShapeDtypeStruct((8, LANES), jnp.float32)],
        in_specs=[anywhere] * len(args),
        out_specs=[pl.BlockSpec(memory_space=pltpu.VMEM)] * (len(rows) + 1),
        scratch_shapes=[pltpu.SemaphoreType.DMA((len(rows), columns // 8))],
        cost_estimate=pl.CostEstimate(
            flops=0, bytes_accessed=4 * len(rows) * columns * channels, transcendentals=0
        ),
        name="copied_rows",
    )(*args)


def whole(body, out_shape, flops, *args, token=None):
    specs = [pl.BlockSpec(memory_space=pltpu.SMEM)]
    specs += [pl.BlockSpec(memory_space=pltpu.VMEM)] * (len(args) - 1)
    if token is not None:
        args += (token,)
        specs.append(pl.BlockSpec(memory_space=pl.ANY))
    return pl.pallas_call(
        body,
        out_shape=out_shape,
        in_specs=specs,
        out_specs=pl.BlockSpec(memory_space=pltpu.VMEM),
        compiler_params=pltpu.CompilerParams(vmem_limit_bytes=10 << 20),
        cost_estimate=pl.CostEstimate(flops=flops, bytes_accessed=3 << 20, transcendentals=0),
        name=body.__name__,
    )(*args)


def exchange(value, axis, flip):
    return lax.ppermute(value, axis, [(i, i ^ flip) for i in range(lax.axis_size(axis))])


def ahead(value, axis, steps, wrap=False):
    count = lax.axis_size(axis)
    pairs = [(i, (i + steps) % count) for i in range(count) if wrap or 0 <= i + steps < count]
    return lax.ppermute(value, axis, pairs)


def per_device(
    query_tokens, key_tokens, value_tokens, norm_gain, hidden, time_weight, space_weight, conv_bias
):
    frames, rows, columns, width = query_tokens.shape
    tokens = frames * rows * columns
    channels = hidden.shape[3]
    frame_axes = ("z", "x")
    row = lax.axis_index("row").astype(jnp.int32).reshape(1)
    x = lax.axis_index("x")
    narrow = lambda value: value.astype(jnp.bfloat16)
    wide = lambda value: value.astype(jnp.float32)

    weights = time_weight, space_weight, conv_bias[None]
    prev_first, prev_last, token = copied_rows(hidden, frames - 1, (0, rows - 1))
    prev_first, prev_last = ahead(prev_first, frame_axes, 1), ahead(prev_last, frame_axes, 1)
    partial = whole(
        partial_kernel,
        jax.ShapeDtypeStruct((SHARES * SHARE_ROWS, LANES), jnp.bfloat16),
        2 * tokens * width * 256,
        row,
        key_tokens.reshape(tokens, width),
        value_tokens.reshape(tokens, width),
        token=token,
    )
    held = partial.reshape(2, 4, SHARE_ROWS, LANES)
    held = wide(held[0]) + wide(exchange(held[1], "row", 1))
    held = held[:2] + wide(exchange(narrow(held[2:]), "row", 2))
    held = held[0] + wide(exchange(narrow(held[1]), "row", 4))

    planes = lax.axis_size("z")
    fold = [(z * INNER + INNER - 1, z * INNER + INNER - 2) for z in range(planes)]
    column = held + wide(lax.ppermute(narrow(held), frame_axes, fold))
    before = jnp.zeros_like(held)
    for k in (1, 2, 4):
        sent = narrow(column)
        if k == 2:
            sent, prev_first = lax.optimization_barrier((sent, prev_first))
        if k == 2:
            up_edge, down_edge, edge_token = edges(hidden, frames - 1, (), time_weight, sent)
            top, bottom = ahead(down_edge, "row", 1), ahead(up_edge, "row", -1)
            ffn_out = conv_frame(hidden, frames - 1, (), top, bottom, weights)
            sent, prev_first, edge_token = lax.optimization_barrier((sent, prev_first, edge_token))
        if k == 4:
            prev_middle, copy_token = copied_rows(hidden, frames - 1, (1,), sent, edge_token)
        pairs = [
            (z * INNER + at, (z + k) * INNER + at)
            for z in range(planes - k)
            for at in range(INNER - 1)
        ]
        arrived = lax.ppermute(sent, frame_axes, pairs)
        column = column + wide(arrived)
        before = before + wide(arrived)
    prefix = before + held
    closed, opened, prev_last, copy_token = lax.optimization_barrier(
        (narrow(prefix), narrow(before), prev_last, copy_token)
    )
    for k in range(1, INNER):
        sent = jnp.where(x + k < INNER, closed, opened)
        prefix = prefix + wide(ahead(sent, "x", k, True))
    prefix = narrow(prefix)
    prev_middle = ahead(lax.optimization_barrier((prev_middle, prefix))[0], frame_axes, 1)
    up_edge, down_edge, _ = edges(hidden, 0, (prev_first, prev_last), time_weight, prefix, copy_token)
    top_first, bottom_first = ahead(down_edge, "row", 1), ahead(up_edge, "row", -1)

    state = jnp.concatenate([prefix, exchange(prefix, "row", 4)], axis=0)
    state = jnp.concatenate([state, exchange(state, "row", 2)], axis=0)
    state, prev_middle, ffn_out = lax.optimization_barrier((state, prev_middle, ffn_out))
    state = jnp.concatenate([state, exchange(state, "row", 1)], axis=0)
    attention = whole(
        mixed_kernel,
        jax.ShapeDtypeStruct((tokens, width), jnp.bfloat16),
        2 * tokens * width * 256,
        row,
        query_tokens.reshape(tokens, width),
        state,
        norm_gain[None],
    )
    ffn_out = conv_frame(
        hidden, 0, (prev_first, prev_middle, prev_last), top_first, bottom_first, weights, ffn_out
    )
    return (attention.reshape(query_tokens.shape), ffn_out)


def solution(mesh):
    frame, row = mesh.shape["frame"], mesh.shape["row"]
    split = Mesh(mesh.devices.reshape(frame // INNER, INNER, row), ("z", "x", "row"))
    tokens = P(("z", "x"), "row", None, None)
    return jax.shard_map(
        per_device,
        mesh=split,
        in_specs=(tokens, tokens, tokens, P(), tokens, P(), P(), P()),
        out_specs=(tokens, tokens),
        check_vma=False,
    )
```

```python
import functools

import jax
import jax.numpy as jnp
from jax import lax
from jax.experimental import pallas as pl
from jax.experimental.pallas import tpu as pltpu
from jax.sharding import Mesh, PartitionSpec as P

HD = 112
FF = 5600
LANES = 128
UNIT = 16
SHARES = 8
SHARE_ROWS = 256
INNER = 4
PARTS = 4
epsilon = 1e-06


def windows(width):
    out = []
    for head in range(width // HD):
        tile, offset = divmod(head * HD, LANES)
        span = LANES if offset + HD <= LANES else 2 * LANES
        out.append((tile, offset, min(span, width - tile * LANES)))
    return out


def unit_row(unit, row):
    share, inside = divmod(unit, UNIT)
    place = share ^ row
    place = ((place & 1) << 2) | (place & 2) | (place >> 2)
    return pl.multiple_of(place * SHARE_ROWS + inside * UNIT, UNIT)


def partial_kernel(row_ref, key_ref, value_ref, token_ref, out_ref):
    row = row_ref[0]
    width = key_ref.shape[1]
    pending = {}

    def flush(tile):
        rounded = pending.pop(tile).astype(jnp.bfloat16)
        for piece in range(HD // UNIT):
            out_ref[pl.ds(unit_row(tile * (HD // UNIT) + piece, row), UNIT), :] = rounded[
                piece * UNIT : (piece + 1) * UNIT
            ]

    for tile, offset, span in windows(width):
        lanes = slice(tile * LANES, tile * LANES + span)
        keys = jnp.maximum(key_ref[:, lanes], 0)
        product = lax.dot_general(
            keys, value_ref[:, lanes], (((0,), (0,)), ((), ())), preferred_element_type=jnp.float32
        )
        block = product[offset : offset + HD]
        lane = lax.broadcasted_iota(jnp.int32, block.shape, 1)
        block = jnp.where((lane >= offset) & (lane < offset + HD), block, 0.0)
        for old in [done for done in pending if done < tile]:
            flush(old)
        for step in range(pl.cdiv(span, LANES)):
            part = block[:, step * LANES : min(span, (step + 1) * LANES)]
            if part.shape[1] < LANES:
                part = jnp.concatenate(
                    [part, jnp.zeros((HD, LANES - part.shape[1]), jnp.float32)], axis=1
                )
            at = tile + step
            pending[at] = pending[at] + part if at in pending else part
    tiles = max(pending) + 1
    for old in sorted(pending):
        flush(old)
    for unit in range(tiles * (HD // UNIT), SHARES * UNIT):
        out_ref[pl.ds(unit_row(unit, row), UNIT), :] = jnp.zeros((UNIT, LANES), jnp.bfloat16)


def mixed_kernel(row_ref, query_ref, state_ref, gain_ref, out_ref):
    row = row_ref[0]
    tokens, width = query_ref.shape
    pending = {}

    def state_tile(tile):
        return jnp.concatenate(
            [
                state_ref[pl.ds(unit_row(tile * (HD // UNIT) + piece, row), UNIT), :]
                for piece in range(HD // UNIT)
            ],
            axis=0,
        )

    def flush(tile):
        lanes = slice(tile * LANES, min(width, (tile + 1) * LANES))
        count = lanes.stop - lanes.start
        out_ref[:, lanes] = (pending.pop(tile)[:, :count] * gain_ref[:, lanes]).astype(jnp.bfloat16)

    for tile, offset, span in windows(width):
        lanes = slice(tile * LANES, tile * LANES + span)
        steps = pl.cdiv(span, LANES)
        block = jnp.concatenate([state_tile(tile + step) for step in range(steps)], axis=1)
        lane = lax.broadcasted_iota(jnp.int32, block.shape, 1)
        block = jnp.where((lane >= offset) & (lane < offset + HD), block, jnp.zeros_like(block))
        pieces = [block]
        if offset:
            pieces.insert(0, jnp.zeros((offset, block.shape[1]), jnp.bfloat16))
        if span - offset - HD:
            pieces.append(jnp.zeros((span - offset - HD, block.shape[1]), jnp.bfloat16))
        right = jnp.concatenate(pieces, axis=0) if len(pieces) > 1 else block
        mixed = jnp.dot(
            jnp.maximum(query_ref[:, lanes], 0), right, preferred_element_type=jnp.float32
        )
        mean_square = jnp.sum(mixed * mixed, axis=1, keepdims=True) * (1.0 / HD)
        normed = mixed * lax.rsqrt(mean_square + epsilon)
        for old in [done for done in pending if done < tile]:
            flush(old)
        for step in range(steps):
            part = normed[:, step * LANES : (step + 1) * LANES]
            at = tile + step
            pending[at] = pending[at] + part if at in pending else part
    for old in sorted(pending):
        flush(old)


def conv_kernel(frame, own_ref, *refs):
    *_, out_ref, held_ref, done_ref, sems, held_sems = refs
    if frame:
        prev_refs = [held_ref.at[0, r] for r in range(own_ref.shape[1])]
    else:
        prev_refs, refs = [ref.at[0] for ref in refs[:3]], refs[3:]
    top_ref, bottom_ref, time_ref, space_ref, bias_ref = refs[:5]
    cur_ref = held_ref.at[-1 % held_ref.shape[0]]
    rows, columns, channels = cur_ref.shape
    groups = columns // 8
    skew = FF % LANES
    lead = FF // LANES
    bounds = [0, lead // 14, lead // 4, lead * 5 // 8, lead]
    fetches = []
    for part, (start, stop) in enumerate(zip(bounds, bounds[1:])):
        gate_start = lead + start + (part > 0)
        gate_stop = min(channels, (lead + stop + 1) * LANES) if part < PARTS - 1 else channels
        spans = (start * LANES, stop * LANES), (gate_start * LANES, gate_stop)
        fetches.append(
            [
                pltpu.make_async_copy(
                    own_ref.at[pl.ds(0, held_ref.shape[0]), :, :, pl.ds(a, b - a)],
                    held_ref.at[:, :, :, pl.ds(a, b - a)],
                    held_sems.at[part, which],
                )
                for which, (a, b) in enumerate(spans)
            ]
        )
        for fetch in fetches[-1]:
            fetch.start()

    def conv_tile(lanes):
        times = time_ref[:, lanes]
        lines = [times[0:1], times[1:2]]
        for a in range(3):
            taps = space_ref[a, :, lanes]
            lines += [taps[b : b + 1] for b in range(3)]
        lines.append(bias_ref[:, lanes])
        shape = (8, lines[0].shape[1])
        pick = [jnp.broadcast_to(line, shape) for line in lines]
        subrow = lax.broadcasted_iota(jnp.int32, shape, 0)
        first, last = subrow == 0, subrow == 7
        zero = jnp.zeros(shape, jnp.float32)

        def split(value):
            return [value[8 * g : 8 * g + 8] for g in range(groups)]

        spread = [split(top_ref[0, :, lanes].astype(jnp.float32))]
        for r in range(rows):
            now = split(cur_ref[r, :, lanes].astype(jnp.float32))
            old = split(prev_refs[r][:, lanes].astype(jnp.float32))
            blend = jnp.concatenate([pick[0] * c + pick[1] * p for c, p in zip(now, old)], axis=0)
            spread.append(split(blend.astype(jnp.bfloat16).astype(jnp.float32)))
        spread.append(split(bottom_ref[0, :, lanes].astype(jnp.float32)))
        out = []
        for r in range(rows):
            sums = []
            for b in range(3):
                sums.append(
                    [
                        pick[2 + b] * spread[r][g]
                        + pick[5 + b] * spread[r + 1][g]
                        + pick[8 + b] * spread[r + 2][g]
                        for g in range(groups)
                    ]
                )
            left = [zero] + [pltpu.roll(value, 1, 0) for value in sums[0]]
            right = [pltpu.roll(value, 7, 0) for value in sums[2]] + [zero]
            out += [
                (pick[11] + sums[1][g])
                + jnp.where(first, left[g], left[g + 1])
                + jnp.where(last, right[g + 1], right[g])
                for g in range(groups)
            ]
        return out

    lane = lax.broadcasted_iota(jnp.int32, (8, LANES), 1)

    def gates(lanes):
        turned = []
        for value in conv_tile(lanes):
            value = value * (1.0 / (1.0 + jnp.exp(-value)))
            if value.shape[1] < LANES:
                rest = jnp.zeros((8, LANES - value.shape[1]), jnp.float32)
                value = jnp.concatenate([value, rest], axis=1)
            turned.append(pltpu.roll(value, LANES - skew, 1))
        return turned

    def step(lanes, near, far, width):
        values = conv_tile(lanes)
        gated = [
            value * jnp.where(lane < LANES - skew, a, b) for value, a, b in zip(values, near, far)
        ]
        for r in range(rows):
            row = jnp.concatenate(gated[r * groups : (r + 1) * groups], axis=0)
            row = row.astype(jnp.bfloat16)
            done_ref[r, :, pl.ds(lanes.start, width)] = row[:, :width]

    def tile_at(index):
        return pl.ds(pl.multiple_of(index * LANES, LANES), LANES)

    def body(tile, near):
        far = gates(tile_at(tile + lead + 1))
        step(tile_at(tile), near, far, LANES)
        return far

    near = None
    for part, (start, stop) in enumerate(zip(bounds, bounds[1:])):
        for fetch in fetches[part]:
            fetch.wait()
        if near is None:
            near = gates(pl.ds(lead * LANES, LANES))
        pairs = (stop - start) // 2

        def pair(at, near, start=start):
            return body(start + 2 * at + 1, body(start + 2 * at, near))

        near = lax.fori_loop(0, pairs, pair, near)
        for tile in range(start + 2 * pairs, stop):
            near = body(tile, near)
    last = (lead * 2 + 1) * LANES
    far = gates(pl.ds(last, channels - last))
    step(pl.ds(lead * LANES, LANES), near, far, skew)
    copies = [
        pltpu.make_async_copy(done_ref.at[r], out_ref.at[frame, r], sems.at[r]) for r in range(rows)
    ]
    for copy in copies:
        copy.start()
    for copy in copies:
        copy.wait()


def conv_frame(hidden, frame, prev, top, bottom, weights, into=None):
    frames, rows, columns, channels = hidden.shape
    args = [hidden, *prev, top, bottom, *weights]
    specs = [pl.BlockSpec(memory_space=pltpu.VMEM)] * len(args)
    args[0] = pltpu.with_memory_space_constraint(hidden, pltpu.HBM)
    specs[0] = pl.BlockSpec(memory_space=pl.ANY)
    aliases = {}
    if into is not None:
        aliases = {len(args): 0}
        args.append(into)
        specs.append(pl.BlockSpec(memory_space=pl.ANY))
    elements = rows * columns * channels
    return pl.pallas_call(
        functools.partial(conv_kernel, frame),
        out_shape=jax.ShapeDtypeStruct((frames, rows, columns, FF), jnp.bfloat16),
        in_specs=specs,
        out_specs=pl.BlockSpec(memory_space=pl.ANY),
        scratch_shapes=[
            pltpu.VMEM((frame + 1, rows, columns, channels), jnp.bfloat16),
            pltpu.VMEM((rows, columns, FF), jnp.bfloat16),
            pltpu.SemaphoreType.DMA((rows,)),
            pltpu.SemaphoreType.DMA((PARTS, 2)),
        ],
        input_output_aliases=aliases,
        compiler_params=pltpu.CompilerParams(vmem_limit_bytes=12 << 20),
        cost_estimate=pl.CostEstimate(
            flops=elements * 40, bytes_accessed=elements * 6, transcendentals=elements // 2
        ),
        name="conv_frame",
    )(*args)


def row_copies(source_ref, target_ref, sems):
    return [
        pltpu.make_async_copy(
            source_ref.at[pl.ds(8 * g, 8)], target_ref.at[pl.ds(8 * g, 8)], sems.at[g]
        )
        for g in range(source_ref.shape[0] // 8)
    ]


def edge_kernel(own_ref, *refs, frame):
    up_ref, down_ref, token_ref, now_ref, old_ref, sems = refs[-6:]
    old_refs, time_ref = (refs[:0], refs[0]) if frame else (refs[:2], refs[2])
    token_ref[...] = jnp.zeros_like(token_ref)
    rows, channels = own_ref.shape[1], own_ref.shape[3]
    ends = (0, rows - 1)
    copies = []
    for at, r in enumerate(ends):
        group = row_copies(own_ref.at[frame, r], now_ref.at[at], sems.at[0, at])
        if frame:
            group += row_copies(own_ref.at[frame - 1, r], old_ref.at[at], sems.at[1, at])
        copies.append(group)
    for copy in copies[0] + copies[1]:
        copy.start()

    for at, out_ref in enumerate((up_ref, down_ref)):
        old_view = old_ref.at[at] if frame else old_refs[at].at[0]
        for copy in copies[at]:
            copy.wait()

        def blend(lanes):
            times = time_ref[:, lanes]
            now = now_ref[at, :, lanes].astype(jnp.float32)
            old = old_view[:, lanes].astype(jnp.float32)
            out_ref[0, :, lanes] = (times[0:1] * now + times[1:2] * old).astype(jnp.bfloat16)

        wide = 4 * LANES

        @pl.loop(0, channels // wide)
        def _(tile):
            blend(pl.ds(pl.multiple_of(tile * wide, LANES), wide))

        if channels % wide:
            blend(pl.ds(channels // wide * wide, channels % wide))


def edges(hidden, frame, old, times, *waits):
    channels, columns = hidden.shape[3], hidden.shape[2]
    held = pl.BlockSpec(memory_space=pltpu.VMEM)
    anywhere = pl.BlockSpec(memory_space=pl.ANY)
    args = [pltpu.with_memory_space_constraint(hidden, pltpu.HBM), *old, times, *waits]
    line = jax.ShapeDtypeStruct((1, columns, channels), jnp.bfloat16)
    pair = pltpu.VMEM((2, columns, channels), jnp.bfloat16)
    return pl.pallas_call(
        functools.partial(edge_kernel, frame=frame),
        out_shape=(line, line, jax.ShapeDtypeStruct((8, LANES), jnp.float32)),
        in_specs=[anywhere] + [held] * (len(old) + 1) + [anywhere] * len(waits),
        out_specs=(held, held, held),
        scratch_shapes=[pair, pair, pltpu.SemaphoreType.DMA((2, 2, columns // 8))],
        compiler_params=pltpu.CompilerParams(vmem_limit_bytes=8 << 20),
        cost_estimate=pl.CostEstimate(
            flops=6 * columns * channels, bytes_accessed=12 * columns * channels, transcendentals=0
        ),
        name="edges",
    )(*args)


def copy_kernel(source_ref, *refs, frame, rows):
    *_, token_ref, sems = refs
    outs = refs[-2 - len(rows) : -2]
    copies = []
    for at, (r, out_ref) in enumerate(zip(rows, outs)):
        copies += row_copies(source_ref.at[frame, r], out_ref.at[0], sems.at[at])
    for copy in copies:
        copy.start()
    token_ref[...] = jnp.zeros_like(token_ref)
    for copy in copies:
        copy.wait()


def copied_rows(hidden, frame, rows, *tokens):
    _, _, columns, channels = hidden.shape
    args = (pltpu.with_memory_space_constraint(hidden, pltpu.HBM), *tokens)
    anywhere = pl.BlockSpec(memory_space=pl.ANY)
    return pl.pallas_call(
        functools.partial(copy_kernel, frame=frame, rows=rows),
        out_shape=[jax.ShapeDtypeStruct((1, columns, channels), jnp.bfloat16) for _ in rows]
        + [jax.ShapeDtypeStruct((8, LANES), jnp.float32)],
        in_specs=[anywhere] * len(args),
        out_specs=[pl.BlockSpec(memory_space=pltpu.VMEM)] * (len(rows) + 1),
        scratch_shapes=[pltpu.SemaphoreType.DMA((len(rows), columns // 8))],
        cost_estimate=pl.CostEstimate(
            flops=0, bytes_accessed=4 * len(rows) * columns * channels, transcendentals=0
        ),
        name="copied_rows",
    )(*args)


def whole(body, out_shape, flops, *args, token=None):
    specs = [pl.BlockSpec(memory_space=pltpu.SMEM)]
    specs += [pl.BlockSpec(memory_space=pltpu.VMEM)] * (len(args) - 1)
    if token is not None:
        args += (token,)
        specs.append(pl.BlockSpec(memory_space=pl.ANY))
    return pl.pallas_call(
        body,
        out_shape=out_shape,
        in_specs=specs,
        out_specs=pl.BlockSpec(memory_space=pltpu.VMEM),
        compiler_params=pltpu.CompilerParams(vmem_limit_bytes=10 << 20),
        cost_estimate=pl.CostEstimate(flops=flops, bytes_accessed=3 << 20, transcendentals=0),
        name=body.__name__,
    )(*args)


def exchange(value, axis, flip):
    return lax.ppermute(value, axis, [(i, i ^ flip) for i in range(lax.axis_size(axis))])


def ahead(value, axis, steps, wrap=False):
    count = lax.axis_size(axis)
    pairs = [(i, (i + steps) % count) for i in range(count) if wrap or 0 <= i + steps < count]
    return lax.ppermute(value, axis, pairs)


def per_device(
    query_tokens, key_tokens, value_tokens, norm_gain, hidden, time_weight, space_weight, conv_bias
):
    frames, rows, columns, width = query_tokens.shape
    tokens = frames * rows * columns
    channels = hidden.shape[3]
    frame_axes = ("z", "x")
    row = lax.axis_index("row").astype(jnp.int32).reshape(1)
    x = lax.axis_index("x")
    narrow = lambda value: value.astype(jnp.bfloat16)
    wide = lambda value: value.astype(jnp.float32)

    weights = time_weight, space_weight, conv_bias[None]
    prev_first, prev_last, token = copied_rows(hidden, frames - 1, (0, rows - 1))
    prev_first, prev_last = ahead(prev_first, frame_axes, 1), ahead(prev_last, frame_axes, 1)
    partial = whole(
        partial_kernel,
        jax.ShapeDtypeStruct((SHARES * SHARE_ROWS, LANES), jnp.bfloat16),
        2 * tokens * width * 256,
        row,
        key_tokens.reshape(tokens, width),
        value_tokens.reshape(tokens, width),
        token=token,
    )
    held = partial.reshape(2, 4, SHARE_ROWS, LANES)
    held = wide(held[0]) + wide(exchange(held[1], "row", 1))
    held = held[:2] + wide(exchange(narrow(held[2:]), "row", 2))
    sent = narrow(held[1])
    up_edge, down_edge, edge_token = edges(hidden, frames - 1, (), time_weight, sent)
    held = held[0] + wide(exchange(sent, "row", 4))

    planes = lax.axis_size("z")
    fold = [(z * INNER + INNER - 1, z * INNER + INNER - 2) for z in range(planes)]
    sent, edge_token = lax.optimization_barrier((narrow(held), edge_token))
    column = held + wide(lax.ppermute(sent, frame_axes, fold))
    before = jnp.zeros_like(held)
    for k in (1, 2, 4):
        sent = narrow(column)
        if k == 2:
            sent, prev_first = lax.optimization_barrier((sent, prev_first))
        if k == 4:
            prev_middle, copy_token = copied_rows(hidden, frames - 1, (1,), sent, edge_token)
        pairs = [
            (z * INNER + at, (z + k) * INNER + at)
            for z in range(planes - k)
            for at in range(INNER - 1)
        ]
        arrived = lax.ppermute(sent, frame_axes, pairs)
        column = column + wide(arrived)
        before = before + wide(arrived)
    prefix = before + held
    top, bottom = ahead(down_edge, "row", 1), ahead(up_edge, "row", -1)
    ffn_out = conv_frame(hidden, frames - 1, (), top, bottom, weights)
    closed, opened, prev_last, copy_token = lax.optimization_barrier(
        (narrow(prefix), narrow(before), prev_last, copy_token)
    )
    for k in range(1, INNER):
        sent = jnp.where(x + k < INNER, closed, opened)
        prefix = prefix + wide(ahead(sent, "x", k, True))
    prefix = narrow(prefix)
    prev_middle = ahead(lax.optimization_barrier((prev_middle, prefix))[0], frame_axes, 1)
    up_edge, down_edge, _ = edges(hidden, 0, (prev_first, prev_last), time_weight, prefix, copy_token)
    top_first, bottom_first = ahead(down_edge, "row", 1), ahead(up_edge, "row", -1)

    state = jnp.concatenate([prefix, exchange(prefix, "row", 4)], axis=0)
    state = jnp.concatenate([state, exchange(state, "row", 2)], axis=0)
    state, prev_middle, ffn_out = lax.optimization_barrier((state, prev_middle, ffn_out))
    state = jnp.concatenate([state, exchange(state, "row", 1)], axis=0)
    attention = whole(
        mixed_kernel,
        jax.ShapeDtypeStruct((tokens, width), jnp.bfloat16),
        2 * tokens * width * 256,
        row,
        query_tokens.reshape(tokens, width),
        state,
        norm_gain[None],
    )
    ffn_out = conv_frame(
        hidden, 0, (prev_first, prev_middle, prev_last), top_first, bottom_first, weights, ffn_out
    )
    return (attention.reshape(query_tokens.shape), ffn_out)


def solution(mesh):
    frame, row = mesh.shape["frame"], mesh.shape["row"]
    split = Mesh(mesh.devices.reshape(frame // INNER, INNER, row), ("z", "x", "row"))
    tokens = P(("z", "x"), "row", None, None)
    return jax.shard_map(
        per_device,
        mesh=split,
        in_specs=(tokens, tokens, tokens, P(), tokens, P(), P(), P()),
        out_specs=(tokens, tokens),
        check_vma=False,
    )
```

```python
import functools

import jax
import jax.numpy as jnp
from jax import lax
from jax.experimental import pallas as pl
from jax.experimental.pallas import tpu as pltpu
from jax.sharding import Mesh, PartitionSpec as P

HD = 112
FF = 5600
LANES = 128
UNIT = 16
SHARES = 8
SHARE_ROWS = 256
INNER = 4
PARTS = 4
epsilon = 1e-06


def windows(width):
    out = []
    for head in range(width // HD):
        tile, offset = divmod(head * HD, LANES)
        span = LANES if offset + HD <= LANES else 2 * LANES
        out.append((tile, offset, min(span, width - tile * LANES)))
    return out


def unit_row(unit, row):
    share, inside = divmod(unit, UNIT)
    place = share ^ row
    place = ((place & 1) << 2) | (place & 2) | (place >> 2)
    return pl.multiple_of(place * SHARE_ROWS + inside * UNIT, UNIT)


def partial_kernel(row_ref, key_ref, value_ref, token_ref, out_ref):
    row = row_ref[0]
    width = key_ref.shape[1]
    pending = {}

    def flush(tile):
        rounded = pending.pop(tile).astype(jnp.bfloat16)
        for piece in range(HD // UNIT):
            out_ref[pl.ds(unit_row(tile * (HD // UNIT) + piece, row), UNIT), :] = rounded[
                piece * UNIT : (piece + 1) * UNIT
            ]

    for tile, offset, span in windows(width):
        lanes = slice(tile * LANES, tile * LANES + span)
        keys = jnp.maximum(key_ref[:, lanes], 0)
        product = lax.dot_general(
            keys, value_ref[:, lanes], (((0,), (0,)), ((), ())), preferred_element_type=jnp.float32
        )
        block = product[offset : offset + HD]
        lane = lax.broadcasted_iota(jnp.int32, block.shape, 1)
        block = jnp.where((lane >= offset) & (lane < offset + HD), block, 0.0)
        for old in [done for done in pending if done < tile]:
            flush(old)
        for step in range(pl.cdiv(span, LANES)):
            part = block[:, step * LANES : min(span, (step + 1) * LANES)]
            if part.shape[1] < LANES:
                part = jnp.concatenate(
                    [part, jnp.zeros((HD, LANES - part.shape[1]), jnp.float32)], axis=1
                )
            at = tile + step
            pending[at] = pending[at] + part if at in pending else part
    tiles = max(pending) + 1
    for old in sorted(pending):
        flush(old)
    for unit in range(tiles * (HD // UNIT), SHARES * UNIT):
        out_ref[pl.ds(unit_row(unit, row), UNIT), :] = jnp.zeros((UNIT, LANES), jnp.bfloat16)


def mixed_kernel(row_ref, query_ref, state_ref, gain_ref, out_ref):
    row = row_ref[0]
    tokens, width = query_ref.shape
    pending = {}

    def state_tile(tile):
        return jnp.concatenate(
            [
                state_ref[pl.ds(unit_row(tile * (HD // UNIT) + piece, row), UNIT), :]
                for piece in range(HD // UNIT)
            ],
            axis=0,
        )

    def flush(tile):
        lanes = slice(tile * LANES, min(width, (tile + 1) * LANES))
        count = lanes.stop - lanes.start
        out_ref[:, lanes] = (pending.pop(tile)[:, :count] * gain_ref[:, lanes]).astype(jnp.bfloat16)

    for tile, offset, span in windows(width):
        lanes = slice(tile * LANES, tile * LANES + span)
        steps = pl.cdiv(span, LANES)
        block = jnp.concatenate([state_tile(tile + step) for step in range(steps)], axis=1)
        lane = lax.broadcasted_iota(jnp.int32, block.shape, 1)
        block = jnp.where((lane >= offset) & (lane < offset + HD), block, jnp.zeros_like(block))
        pieces = [block]
        if offset:
            pieces.insert(0, jnp.zeros((offset, block.shape[1]), jnp.bfloat16))
        if span - offset - HD:
            pieces.append(jnp.zeros((span - offset - HD, block.shape[1]), jnp.bfloat16))
        right = jnp.concatenate(pieces, axis=0) if len(pieces) > 1 else block
        mixed = jnp.dot(
            jnp.maximum(query_ref[:, lanes], 0), right, preferred_element_type=jnp.float32
        )
        mean_square = jnp.sum(mixed * mixed, axis=1, keepdims=True) * (1.0 / HD)
        normed = mixed * lax.rsqrt(mean_square + epsilon)
        for old in [done for done in pending if done < tile]:
            flush(old)
        for step in range(steps):
            part = normed[:, step * LANES : (step + 1) * LANES]
            at = tile + step
            pending[at] = pending[at] + part if at in pending else part
    for old in sorted(pending):
        flush(old)


def conv_kernel(frame, own_ref, *refs):
    *_, out_ref, held_ref, done_ref, sems, held_sems = refs
    if frame:
        prev_refs = [held_ref.at[0, r] for r in range(own_ref.shape[1])]
    else:
        prev_refs, refs = [ref.at[0] for ref in refs[:3]], refs[3:]
    top_ref, bottom_ref, time_ref, space_ref, bias_ref = refs[:5]
    cur_ref = held_ref.at[-1 % held_ref.shape[0]]
    rows, columns, channels = cur_ref.shape
    groups = columns // 8
    skew = FF % LANES
    lead = FF // LANES
    bounds = [0, lead // 14, lead // 4, lead * 5 // 8, lead]
    fetches = []
    for part, (start, stop) in enumerate(zip(bounds, bounds[1:])):
        gate_start = lead + start + (part > 0)
        gate_stop = min(channels, (lead + stop + 1) * LANES) if part < PARTS - 1 else channels
        spans = (start * LANES, stop * LANES), (gate_start * LANES, gate_stop)
        fetches.append(
            [
                pltpu.make_async_copy(
                    own_ref.at[pl.ds(0, held_ref.shape[0]), :, :, pl.ds(a, b - a)],
                    held_ref.at[:, :, :, pl.ds(a, b - a)],
                    held_sems.at[part, which],
                )
                for which, (a, b) in enumerate(spans)
            ]
        )
        for fetch in fetches[-1]:
            fetch.start()

    def conv_tile(lanes):
        times = time_ref[:, lanes]
        lines = [times[0:1], times[1:2]]
        for a in range(3):
            taps = space_ref[a, :, lanes]
            lines += [taps[b : b + 1] for b in range(3)]
        lines.append(bias_ref[:, lanes])
        shape = (8, lines[0].shape[1])
        pick = [jnp.broadcast_to(line, shape) for line in lines]
        subrow = lax.broadcasted_iota(jnp.int32, shape, 0)
        first, last = subrow == 0, subrow == 7
        zero = jnp.zeros(shape, jnp.float32)

        def split(value):
            return [value[8 * g : 8 * g + 8] for g in range(groups)]

        spread = [split(top_ref[0, :, lanes].astype(jnp.float32))]
        for r in range(rows):
            now = split(cur_ref[r, :, lanes].astype(jnp.float32))
            old = split(prev_refs[r][:, lanes].astype(jnp.float32))
            blend = jnp.concatenate([pick[0] * c + pick[1] * p for c, p in zip(now, old)], axis=0)
            spread.append(split(blend.astype(jnp.bfloat16).astype(jnp.float32)))
        spread.append(split(bottom_ref[0, :, lanes].astype(jnp.float32)))
        out = []
        for r in range(rows):
            sums = []
            for b in range(3):
                sums.append(
                    [
                        pick[2 + b] * spread[r][g]
                        + pick[5 + b] * spread[r + 1][g]
                        + pick[8 + b] * spread[r + 2][g]
                        for g in range(groups)
                    ]
                )
            left = [zero] + [pltpu.roll(value, 1, 0) for value in sums[0]]
            right = [pltpu.roll(value, 7, 0) for value in sums[2]] + [zero]
            out += [
                (pick[11] + sums[1][g])
                + jnp.where(first, left[g], left[g + 1])
                + jnp.where(last, right[g + 1], right[g])
                for g in range(groups)
            ]
        return out

    lane = lax.broadcasted_iota(jnp.int32, (8, LANES), 1)

    def gates(lanes):
        turned = []
        for value in conv_tile(lanes):
            value = value * (1.0 / (1.0 + jnp.exp(-value)))
            if value.shape[1] < LANES:
                rest = jnp.zeros((8, LANES - value.shape[1]), jnp.float32)
                value = jnp.concatenate([value, rest], axis=1)
            turned.append(pltpu.roll(value, LANES - skew, 1))
        return turned

    def step(lanes, near, far, width):
        values = conv_tile(lanes)
        gated = [
            value * jnp.where(lane < LANES - skew, a, b) for value, a, b in zip(values, near, far)
        ]
        for r in range(rows):
            row = jnp.concatenate(gated[r * groups : (r + 1) * groups], axis=0)
            row = row.astype(jnp.bfloat16)
            done_ref[r, :, pl.ds(lanes.start, width)] = row[:, :width]

    def tile_at(index):
        return pl.ds(pl.multiple_of(index * LANES, LANES), LANES)

    def body(tile, near):
        far = gates(tile_at(tile + lead + 1))
        step(tile_at(tile), near, far, LANES)
        return far

    near = None
    for part, (start, stop) in enumerate(zip(bounds, bounds[1:])):
        for fetch in fetches[part]:
            fetch.wait()
        if near is None:
            near = gates(pl.ds(lead * LANES, LANES))
        trips = (stop - start) // 4

        def trip(at, near, start=start):
            for tile in range(4):
                near = body(start + 4 * at + tile, near)
            return near

        near = lax.fori_loop(0, trips, trip, near)
        for tile in range(start + 4 * trips, stop):
            near = body(tile, near)
    last = (lead * 2 + 1) * LANES
    far = gates(pl.ds(last, channels - last))
    step(pl.ds(lead * LANES, LANES), near, far, skew)
    copies = [
        pltpu.make_async_copy(done_ref.at[r], out_ref.at[frame, r], sems.at[r]) for r in range(rows)
    ]
    for copy in copies:
        copy.start()
    for copy in copies:
        copy.wait()


def conv_frame(hidden, frame, prev, top, bottom, weights, into=None):
    frames, rows, columns, channels = hidden.shape
    args = [hidden, *prev, top, bottom, *weights]
    specs = [pl.BlockSpec(memory_space=pltpu.VMEM)] * len(args)
    args[0] = pltpu.with_memory_space_constraint(hidden, pltpu.HBM)
    specs[0] = pl.BlockSpec(memory_space=pl.ANY)
    aliases = {}
    if into is not None:
        aliases = {len(args): 0}
        args.append(into)
        specs.append(pl.BlockSpec(memory_space=pl.ANY))
    elements = rows * columns * channels
    return pl.pallas_call(
        functools.partial(conv_kernel, frame),
        out_shape=jax.ShapeDtypeStruct((frames, rows, columns, FF), jnp.bfloat16),
        in_specs=specs,
        out_specs=pl.BlockSpec(memory_space=pl.ANY),
        scratch_shapes=[
            pltpu.VMEM((frame + 1, rows, columns, channels), jnp.bfloat16),
            pltpu.VMEM((rows, columns, FF), jnp.bfloat16),
            pltpu.SemaphoreType.DMA((rows,)),
            pltpu.SemaphoreType.DMA((PARTS, 2)),
        ],
        input_output_aliases=aliases,
        compiler_params=pltpu.CompilerParams(vmem_limit_bytes=12 << 20),
        cost_estimate=pl.CostEstimate(
            flops=elements * 40, bytes_accessed=elements * 6, transcendentals=elements // 2
        ),
        name="conv_frame",
    )(*args)


def row_copies(source_ref, target_ref, sems):
    return [
        pltpu.make_async_copy(
            source_ref.at[pl.ds(8 * g, 8)], target_ref.at[pl.ds(8 * g, 8)], sems.at[g]
        )
        for g in range(source_ref.shape[0] // 8)
    ]


def edge_kernel(own_ref, *refs, frame):
    up_ref, down_ref, token_ref, now_ref, old_ref, sems = refs[-6:]
    old_refs, time_ref = (refs[:0], refs[0]) if frame else (refs[:2], refs[2])
    token_ref[...] = jnp.zeros_like(token_ref)
    rows, channels = own_ref.shape[1], own_ref.shape[3]
    ends = (0, rows - 1)
    copies = []
    for at, r in enumerate(ends):
        group = row_copies(own_ref.at[frame, r], now_ref.at[at], sems.at[0, at])
        if frame:
            group += row_copies(own_ref.at[frame - 1, r], old_ref.at[at], sems.at[1, at])
        copies.append(group)
    for copy in copies[0] + copies[1]:
        copy.start()

    for at, out_ref in enumerate((up_ref, down_ref)):
        old_view = old_ref.at[at] if frame else old_refs[at].at[0]
        for copy in copies[at]:
            copy.wait()

        def blend(lanes):
            times = time_ref[:, lanes]
            now = now_ref[at, :, lanes].astype(jnp.float32)
            old = old_view[:, lanes].astype(jnp.float32)
            out_ref[0, :, lanes] = (times[0:1] * now + times[1:2] * old).astype(jnp.bfloat16)

        wide = 4 * LANES

        @pl.loop(0, channels // wide)
        def _(tile):
            blend(pl.ds(pl.multiple_of(tile * wide, LANES), wide))

        if channels % wide:
            blend(pl.ds(channels // wide * wide, channels % wide))


def edges(hidden, frame, old, times, *waits):
    channels, columns = hidden.shape[3], hidden.shape[2]
    held = pl.BlockSpec(memory_space=pltpu.VMEM)
    anywhere = pl.BlockSpec(memory_space=pl.ANY)
    args = [pltpu.with_memory_space_constraint(hidden, pltpu.HBM), *old, times, *waits]
    line = jax.ShapeDtypeStruct((1, columns, channels), jnp.bfloat16)
    pair = pltpu.VMEM((2, columns, channels), jnp.bfloat16)
    return pl.pallas_call(
        functools.partial(edge_kernel, frame=frame),
        out_shape=(line, line, jax.ShapeDtypeStruct((8, LANES), jnp.float32)),
        in_specs=[anywhere] + [held] * (len(old) + 1) + [anywhere] * len(waits),
        out_specs=(held, held, held),
        scratch_shapes=[pair, pair, pltpu.SemaphoreType.DMA((2, 2, columns // 8))],
        compiler_params=pltpu.CompilerParams(vmem_limit_bytes=8 << 20),
        cost_estimate=pl.CostEstimate(
            flops=6 * columns * channels, bytes_accessed=12 * columns * channels, transcendentals=0
        ),
        name="edges",
    )(*args)


def copy_kernel(source_ref, *refs, frame, rows):
    *_, token_ref, sems = refs
    outs = refs[-2 - len(rows) : -2]
    copies = []
    for at, (r, out_ref) in enumerate(zip(rows, outs)):
        copies += row_copies(source_ref.at[frame, r], out_ref.at[0], sems.at[at])
    for copy in copies:
        copy.start()
    token_ref[...] = jnp.zeros_like(token_ref)
    for copy in copies:
        copy.wait()


def copied_rows(hidden, frame, rows, *tokens):
    _, _, columns, channels = hidden.shape
    args = (pltpu.with_memory_space_constraint(hidden, pltpu.HBM), *tokens)
    anywhere = pl.BlockSpec(memory_space=pl.ANY)
    return pl.pallas_call(
        functools.partial(copy_kernel, frame=frame, rows=rows),
        out_shape=[jax.ShapeDtypeStruct((1, columns, channels), jnp.bfloat16) for _ in rows]
        + [jax.ShapeDtypeStruct((8, LANES), jnp.float32)],
        in_specs=[anywhere] * len(args),
        out_specs=[pl.BlockSpec(memory_space=pltpu.VMEM)] * (len(rows) + 1),
        scratch_shapes=[pltpu.SemaphoreType.DMA((len(rows), columns // 8))],
        cost_estimate=pl.CostEstimate(
            flops=0, bytes_accessed=4 * len(rows) * columns * channels, transcendentals=0
        ),
        name="copied_rows",
    )(*args)


def whole(body, out_shape, flops, *args, token=None):
    specs = [pl.BlockSpec(memory_space=pltpu.SMEM)]
    specs += [pl.BlockSpec(memory_space=pltpu.VMEM)] * (len(args) - 1)
    if token is not None:
        args += (token,)
        specs.append(pl.BlockSpec(memory_space=pl.ANY))
    return pl.pallas_call(
        body,
        out_shape=out_shape,
        in_specs=specs,
        out_specs=pl.BlockSpec(memory_space=pltpu.VMEM),
        compiler_params=pltpu.CompilerParams(vmem_limit_bytes=10 << 20),
        cost_estimate=pl.CostEstimate(flops=flops, bytes_accessed=3 << 20, transcendentals=0),
        name=body.__name__,
    )(*args)


def exchange(value, axis, flip):
    return lax.ppermute(value, axis, [(i, i ^ flip) for i in range(lax.axis_size(axis))])


def ahead(value, axis, steps, wrap=False):
    count = lax.axis_size(axis)
    pairs = [(i, (i + steps) % count) for i in range(count) if wrap or 0 <= i + steps < count]
    return lax.ppermute(value, axis, pairs)


def per_device(
    query_tokens, key_tokens, value_tokens, norm_gain, hidden, time_weight, space_weight, conv_bias
):
    frames, rows, columns, width = query_tokens.shape
    tokens = frames * rows * columns
    channels = hidden.shape[3]
    frame_axes = ("z", "x")
    row = lax.axis_index("row").astype(jnp.int32).reshape(1)
    x = lax.axis_index("x")
    narrow = lambda value: value.astype(jnp.bfloat16)
    wide = lambda value: value.astype(jnp.float32)

    weights = time_weight, space_weight, conv_bias[None]
    prev_first, prev_last, token = copied_rows(hidden, frames - 1, (0, rows - 1))
    prev_first, prev_last = ahead(prev_first, frame_axes, 1), ahead(prev_last, frame_axes, 1)
    partial = whole(
        partial_kernel,
        jax.ShapeDtypeStruct((SHARES * SHARE_ROWS, LANES), jnp.bfloat16),
        2 * tokens * width * 256,
        row,
        key_tokens.reshape(tokens, width),
        value_tokens.reshape(tokens, width),
        token=token,
    )
    held = partial.reshape(2, 4, SHARE_ROWS, LANES)
    held = wide(held[0]) + wide(exchange(held[1], "row", 1))
    held = held[:2] + wide(exchange(narrow(held[2:]), "row", 2))
    sent = narrow(held[1])
    up_edge, down_edge, edge_token = edges(hidden, frames - 1, (), time_weight, sent)
    held = held[0] + wide(exchange(sent, "row", 4))

    planes = lax.axis_size("z")
    fold = [(z * INNER + INNER - 1, z * INNER + INNER - 2) for z in range(planes)]
    sent, edge_token = lax.optimization_barrier((narrow(held), edge_token))
    column = held + wide(lax.ppermute(sent, frame_axes, fold))
    before = jnp.zeros_like(held)
    for k in (1, 2, 4):
        sent = narrow(column)
        if k == 2:
            sent, prev_first = lax.optimization_barrier((sent, prev_first))
        if k == 4:
            prev_middle, copy_token = copied_rows(hidden, frames - 1, (1,), sent, edge_token)
        pairs = [
            (z * INNER + at, (z + k) * INNER + at)
            for z in range(planes - k)
            for at in range(INNER - 1)
        ]
        arrived = lax.ppermute(sent, frame_axes, pairs)
        column = column + wide(arrived)
        before = before + wide(arrived)
    prefix = before + held
    top, bottom = ahead(down_edge, "row", 1), ahead(up_edge, "row", -1)
    ffn_out = conv_frame(hidden, frames - 1, (), top, bottom, weights)
    closed, opened, prev_last, copy_token = lax.optimization_barrier(
        (narrow(prefix), narrow(before), prev_last, copy_token)
    )
    for k in range(1, INNER):
        sent = jnp.where(x + k < INNER, closed, opened)
        prefix = prefix + wide(ahead(sent, "x", k, True))
    prefix = narrow(prefix)
    prev_middle = ahead(lax.optimization_barrier((prev_middle, prefix))[0], frame_axes, 1)
    up_edge, down_edge, _ = edges(hidden, 0, (prev_first, prev_last), time_weight, prefix, copy_token)
    top_first, bottom_first = ahead(down_edge, "row", 1), ahead(up_edge, "row", -1)

    state = jnp.concatenate([prefix, exchange(prefix, "row", 4)], axis=0)
    state = jnp.concatenate([state, exchange(state, "row", 2)], axis=0)
    state, prev_middle, ffn_out = lax.optimization_barrier((state, prev_middle, ffn_out))
    state = jnp.concatenate([state, exchange(state, "row", 1)], axis=0)
    attention = whole(
        mixed_kernel,
        jax.ShapeDtypeStruct((tokens, width), jnp.bfloat16),
        2 * tokens * width * 256,
        row,
        query_tokens.reshape(tokens, width),
        state,
        norm_gain[None],
    )
    ffn_out = conv_frame(
        hidden, 0, (prev_first, prev_middle, prev_last), top_first, bottom_first, weights, ffn_out
    )
    return (attention.reshape(query_tokens.shape), ffn_out)


def solution(mesh):
    frame, row = mesh.shape["frame"], mesh.shape["row"]
    split = Mesh(mesh.devices.reshape(frame // INNER, INNER, row), ("z", "x", "row"))
    tokens = P(("z", "x"), "row", None, None)
    return jax.shard_map(
        per_device,
        mesh=split,
        in_specs=(tokens, tokens, tokens, P(), tokens, P(), P(), P()),
        out_specs=(tokens, tokens),
        check_vma=False,
    )
```
